128 devices in a mesh: row: 8 (over y_hi, x), col: 16 (over z, y_lo, core).
Axes of the slice: x: 4, y: 4 (y_hi: 2, y_lo: 2; y = y_hi * 2 + y_lo), z: 4, core: 2. Of those that a mesh axis runs over, the one named last changes fastest.
Arguments:
- features: bfloat16 [64, 1024, 768], P('row', 'col'), may hold values from -6 to 6
- norm_scale: float32 [768], replicated, may hold values from 0.5 to 1.5
- norm_shift: float32 [768], replicated, may hold values from -3 to 3
- expand_weight: bfloat16 [768, 3072], replicated, may hold values from -0.21875 to 0.21875
- expand_bias: float32 [3072], replicated, may hold values from -3 to 3
- depth_kernel: float32 [3, 3, 3072], replicated, may hold values from -2 to 2
- depth_bias: float32 [3072], replicated, may hold values from -3 to 3
- project_weight: bfloat16 [3072, 768], replicated, may hold values from -0.109375 to 0.109375
- project_bias: float32 [768], replicated, may hold values from -2 to 2
- attn_gain: float32 [768], replicated, may hold values from 0.25 to 1.75
- attn_shift: float32 [768], replicated, may hold values from -2 to 2
- qkv_weight: bfloat16 [768, 2304], replicated, may hold values from -0.21875 to 0.21875
- qkv_bias: float32 [2304], replicated, may hold values from -2 to 2
- out_weight: bfloat16 [768, 768], replicated, may hold values from -0.21875 to 0.21875
- out_bias: float32 [768], replicated, may hold values from -2 to 2
Outputs:
- output: bfloat16 [64, 1024, 768], P('row', 'col')
The draws below stay inside these ranges and needn't reach their ends.
All inputs are finite; a program needn't handle non-finite values.
Results may differ from the reference program's by a relative error of at most 0.006.
Values may be sent and summed in bfloat16 or wider, within the bound.
A program may use at most 192 MiB of HBM per device.

```python
import math
import jax
import jax.numpy as jnp
from jax import lax

C = 768
HEADS = 24
HEAD_DIM = 32
EXPAND = 3072
GRID = 8
H = 64
W = 1024


def block_levels(stream_key, dims, cuts, smallest, high):
    def one(position, parts):
        draws = jax.random.uniform(jax.random.fold_in(jax.random.fold_in(stream_key, 6), position), (parts,), jnp.float32, smallest / len(cuts), high / len(cuts))
        return jnp.repeat(jnp.exp(draws), dims[position] // parts).reshape((-1,) + (1,) * (len(dims) - position - 1))

    gain = one(*cuts[0])
    for cut in cuts[1:]:
        gain = gain * one(*cut)
    return gain


def gaussian(rng, shape, scale, limit, pieces=(), kind=jnp.bfloat16):
    factor_of = block_levels(rng, shape, pieces, -0.22, 0.18) if pieces else 1.0
    values = jax.random.normal(rng, shape, jnp.float32) * scale * factor_of
    return jnp.minimum(jnp.maximum(values, -limit), limit).astype(kind)


def setup_inputs(seed: int = 0) -> dict:
    seeds = jax.random.split(jax.random.key(seed), 16)
    return {
        "features": gaussian(seeds[0], (H, W, C), 1.0, 6.0, ((0, 8), (1, 16))),
        "norm_scale": jnp.clip(1.0 + 0.1 * jax.random.normal(seeds[1], (C,), jnp.float32), 0.5, 1.5),
        "norm_shift": gaussian(seeds[2], (C,), 0.5, 3.0, (), jnp.float32),
        "expand_weight": gaussian(seeds[3], (C, EXPAND), C ** -0.5, 0.21875),
        "expand_bias": gaussian(seeds[4], (EXPAND,), 0.5, 3.0, (), jnp.float32),
        "depth_kernel": gaussian(seeds[5], (3, 3, EXPAND), 9 ** -0.5, 2.0, (), jnp.float32),
        "depth_bias": gaussian(seeds[6], (EXPAND,), 0.5, 3.0, (), jnp.float32),
        "project_weight": gaussian(seeds[7], (EXPAND, C), EXPAND ** -0.5, 0.109375),
        "project_bias": gaussian(seeds[8], (C,), 0.3, 2.0, (), jnp.float32),
        "attn_gain": jnp.clip(1.0 + 0.15 * jax.random.normal(seeds[9], (C,), jnp.float32), 0.25, 1.75),
        "attn_shift": gaussian(seeds[10], (C,), 0.3, 2.0, (), jnp.float32),
        "qkv_weight": gaussian(seeds[11], (C, 3 * C), C ** -0.5, 0.21875),
        "qkv_bias": gaussian(seeds[12], (3 * C,), 0.3, 2.0, (), jnp.float32),
        "out_weight": gaussian(seeds[13], (C, C), C ** -0.5, 0.21875),
        "out_bias": gaussian(seeds[14], (C,), 0.3, 2.0, (), jnp.float32),
    }


def layer_norm(values, scale_vec, shift_vec):
    widened = values.astype(jnp.float32)
    center = widened - lax.optimization_barrier(jnp.mean(widened, axis=-1, keepdims=True))
    spread = lax.optimization_barrier(jnp.mean(center * center, axis=-1, keepdims=True))
    return (center * lax.rsqrt(spread + 1e-06) * scale_vec + shift_vec).astype(jnp.bfloat16)

def attend(tokens_in, pattern, qkv_weight, qkv_bias, out_weight, out_bias):
    channels = tokens_in.shape[-1]
    leading = tokens_in.shape[:-1]
    projected = jnp.dot(tokens_in.reshape(-1, channels), qkv_weight, preferred_element_type=jnp.float32) + qkv_bias
    projected = projected.astype(jnp.bfloat16).reshape(leading + (3, HEADS, HEAD_DIM))
    query_part = projected[..., 0, :, :].astype(jnp.float32)
    key_part = projected[..., 1, :, :].astype(jnp.float32)
    value_part = projected[..., 2, :, :].astype(jnp.float32)
    renamed = {'i': 'm', 'j': 'n', 'k': 'o', 'l': 'p'}
    token_letters = 'ijkl'
    key_pattern = ''.join((renamed.get(letter, letter) for letter in pattern))
    groups = ''.join((letter for letter in pattern if letter not in token_letters))
    query_tokens = ''.join((letter for letter in pattern if letter in token_letters))
    key_tokens = ''.join((renamed[letter] for letter in query_tokens))
    score_form = groups + 'h' + query_tokens + key_tokens
    scores = jnp.einsum(pattern + 'hd,' + key_pattern + 'hd->' + score_form, query_part, key_part) * (1.0 / math.sqrt(HEAD_DIM))
    weights = jnp.exp(scores)
    total = lax.optimization_barrier(jnp.sum(weights, axis=tuple(range(-len(key_tokens), 0)), keepdims=True))
    probs = (weights / total).astype(jnp.bfloat16)
    mixed = jnp.einsum(score_form + ',' + key_pattern + 'hd->' + pattern + 'hd', probs.astype(jnp.float32), value_part)
    mixed = mixed.astype(jnp.bfloat16)
    result = jnp.dot(mixed.reshape(-1, channels), out_weight, preferred_element_type=jnp.float32) + out_bias
    return result.astype(jnp.bfloat16).reshape(tokens_in.shape)

def reference(features, norm_scale, norm_shift, expand_weight, expand_bias, depth_kernel, depth_bias, project_weight, project_bias, attn_gain, attn_shift, qkv_weight, qkv_bias, out_weight, out_bias):
    normed = (features.astype(jnp.float32) * norm_scale + norm_shift).astype(jnp.bfloat16)

    def expand_row(row_in):
        return jax.nn.gelu(jnp.dot(row_in, expand_weight, preferred_element_type=jnp.float32) + expand_bias).astype(jnp.bfloat16)
    hidden = lax.map(expand_row, normed)
    padded = jnp.pad(hidden, ((1, 1), (1, 1), (0, 0)))

    def convolve_row(pair):
        row_index, row_in = pair
        window = lax.dynamic_slice_in_dim(padded, row_index, 3, 0)
        summed = jnp.zeros((W, EXPAND), jnp.float32)
        for row_off in range(3):
            for col_off in range(3):
                summed = summed + window[row_off, col_off:col_off + W].astype(jnp.float32) * depth_kernel[row_off, col_off]
        depthwise = jax.nn.gelu(summed + depth_bias).astype(jnp.bfloat16)
        projected = jnp.dot(depthwise, project_weight, preferred_element_type=jnp.float32) + project_bias
        return (row_in.astype(jnp.float32) + projected).astype(jnp.bfloat16)
    after_conv = lax.map(convolve_row, (jnp.arange(H, dtype=jnp.int32), features))
    attn_in = layer_norm(after_conv, attn_gain, attn_shift)
    stride_rows = H // GRID
    stride_cols = W // GRID
    split_view = attn_in.reshape(GRID, stride_rows, GRID, stride_cols, C).transpose(1, 0, 2, 3, 4)

    def attend_slice(piece):
        return attend(piece, 'jlv', qkv_weight, qkv_bias, out_weight, out_bias)
    answered = lax.map(attend_slice, split_view)
    attended = answered.transpose(1, 0, 2, 3, 4).reshape(H, W, C)
    return (after_conv.astype(jnp.float32) + attended.astype(jnp.float32)).astype(jnp.bfloat16)
```

```python
import math

import jax
import jax.numpy as jnp
from jax import lax
from jax.experimental import pallas as pl
from jax.experimental.pallas import tpu as pltpu
from jax.sharding import PartitionSpec as P

MESH = pl.DeviceIdType.MESH
F32 = jnp.float32
BF16 = jnp.bfloat16

ROWS, COLS = 8, 16
PEERS = 64
TR, TC = 8, 64
TOKENS = TR * TC
C = 768
E = 3072
HEAD_DIM = 32
QUADS = 6
NQ = 2
WCHUNKS = 6
GC1 = math.sqrt(2.0 / math.pi)
GC2 = GC1 * 0.044715
EXP_SCALE = math.log2(math.e) / math.sqrt(HEAD_DIM)


def gelu(v):
    half = 0.5 * v
    return half + half * jnp.tanh(v * (GC1 + GC2 * (v * v)))


def kernel(
    f_hbm, nsc_h, nsh_h, we_h, be_h, dk_h, db_h, wp_h, bp_h, ag_h, as_h, wq_h, bq_h, wo_h, bo_h,
    ac_out, ret_out,
    feat, nsc, nsh, we, be, dk, db, wp, bp, ag, ash, wq, bq, wo, bo,
    xn, top, bot, left, right, corner, xblk, xcol, hid, hl, hr, dwb, send, recv, xp, qkv, mixed, retbuf, ones,
    small_sem, feat_sem, we_sem, w_sem, halo_ssem, halo_rsem, a_ssem, a_rsem, b_ssem, b_rsem, out_sem, self_sem,
):
    r = lax.axis_index("row")
    c = lax.axis_index("col")
    core = lax.rem(c, 2)
    me = r * 8 + c // 2

    def place(p):
        return (p // 8, 2 * lax.rem(p, 8) + core)

    bar = pltpu.get_barrier_semaphore()

    fcopy = pltpu.make_async_copy(f_hbm, feat, feat_sem)
    fcopy.start()
    smalls = [
        pltpu.make_async_copy(s, d, small_sem.at[i])
        for i, (s, d) in enumerate(
            ((nsc_h, nsc), (nsh_h, nsh), (be_h, be), (dk_h, dk), (db_h, db), (bp_h, bp),
             (ag_h, ag), (as_h, ash), (bq_h, bq), (bo_h, bo))
        )
    ]
    for s in smalls:
        s.start()
    wide = E // WCHUNKS
    wcopies = [
        pltpu.make_async_copy(
            we_h.at[:, pl.ds(i * wide, wide)], we.at[:, pl.ds(i * wide, wide)], we_sem.at[i]
        )
        for i in range(WCHUNKS)
    ]
    for w in wcopies:
        w.start()

    def signal(i, _):
        pl.semaphore_signal(
            bar, inc=1, device_id=place(lax.rem(me + i, PEERS)), device_id_type=MESH
        )
        return 0

    lax.fori_loop(1, PEERS, signal, 0)
    for dr in (-1, 0, 1):
        for dc in (-1, 1):
            pl.semaphore_signal(
                bar, inc=1,
                device_id=(lax.rem(r + dr + ROWS, ROWS), lax.rem(c + dc + COLS, COLS)),
                device_id_type=MESH,
            )

    bigs = [
        pltpu.make_async_copy(s, d, w_sem.at[i])
        for i, (s, d) in enumerate(((wp_h, wp), (wq_h, wq), (wo_h, wo)))
    ]
    for w in bigs:
        w.start()

    fcopy.wait()
    for s in smalls:
        s.wait()

    def normalise(v):
        return (v.astype(F32) * nsc[...] + nsh[...]).astype(BF16)

    def norm_row(h, _):
        xn[pl.ds(pl.multiple_of(h * TC, TC), TC), :] = normalise(feat[h])
        return 0

    lax.fori_loop(0, TR, norm_row, 0)

    def expand_chunk(ci, _):
        cols = pl.ds(pl.multiple_of(ci * 256, 256), 256)
        for mb in range(2):
            acc = jnp.dot(
                xn[mb * 256 : (mb + 1) * 256, :], we[:, cols], preferred_element_type=F32
            )
            g = gelu(acc + be[:, cols]).astype(BF16)
            hid[1 + 4 * mb : 5 + 4 * mb, :, cols] = g.reshape(4, TC, 256)
        return 0

    early = 4
    for i in range(early):
        wcopies[i].wait()
        lax.fori_loop(2 * i, 2 * i + 2, expand_chunk, 0)

    pl.semaphore_wait(bar, PEERS - 1 + 6)

    def halo(src, dst, k, dr, dc):
        return pltpu.make_async_remote_copy(
            src_ref=src, dst_ref=dst, send_sem=halo_ssem.at[k], recv_sem=halo_rsem.at[k],
            device_id=(lax.rem(r + dr + ROWS, ROWS), lax.rem(c + dc + COLS, COLS)),
            device_id_type=MESH,
        )

    halos = [
        halo(feat.at[TR - 1], top, 0, 1, 0),
        halo(feat.at[0], bot, 1, -1, 0),
        halo(feat.at[:, pl.ds(TC - 8, 8)], left, 2, 0, 1),
        halo(feat.at[:, pl.ds(0, 8)], right, 3, 0, -1),
        halo(feat.at[TR - 1, pl.ds(TC - 8, 8)], corner.at[0], 4, 1, 1),
        halo(feat.at[0, pl.ds(TC - 8, 8)], corner.at[1], 5, -1, 1),
        halo(feat.at[TR - 1, pl.ds(0, 8)], corner.at[2], 6, 1, -1),
        halo(feat.at[0, pl.ds(0, 8)], corner.at[3], 7, -1, -1),
    ]
    for h in halos:
        h.start()

    for i in range(early, WCHUNKS):
        wcopies[i].wait()
        lax.fori_loop(2 * i, 2 * i + 2, expand_chunk, 0)

    for h in halos:
        h.wait()

    top_ok = jnp.where(r > 0, 1.0, 0.0).astype(F32)
    bot_ok = jnp.where(r < ROWS - 1, 1.0, 0.0).astype(F32)
    left_ok = jnp.where(c > 0, 1.0, 0.0).astype(F32)
    right_ok = jnp.where(c < COLS - 1, 1.0, 0.0).astype(F32)

    xn[0:TC, :] = normalise(top[...])
    xn[TC : 2 * TC, :] = normalise(bot[...])
    for i in range(TR):
        xblk[i * 8 : i * 8 + 8, :] = normalise(left[i])
        xblk[64 + i * 8 : 64 + i * 8 + 8, :] = normalise(right[i])
    for i in range(4):
        xblk[128 + i * 8 : 136 + i * 8, :] = normalise(corner[i])
    xblk[160:256, :] = jnp.zeros((96, C), BF16)
    t = lax.broadcasted_iota(jnp.int32, (32, 256), 0)
    n = lax.broadcasted_iota(jnp.int32, (32, 256), 1)
    tr = lax.rem(t, 16)
    want_l = jnp.where(tr == 0, 135, jnp.where(tr == 9, 143, (tr - 1) * 8 + 7))
    want_r = jnp.where(tr == 0, 144, jnp.where(tr == 9, 152, 64 + (tr - 1) * 8))
    want = jnp.where(t < 16, want_l, want_r)
    want = jnp.where(tr <= 9, want, -1)
    pick = jnp.where(n == want, 1.0, 0.0).astype(BF16)
    xcol[...] = jnp.dot(pick, xblk[...], preferred_element_type=F32).astype(BF16)

    def halo_chunk(ci, _):
        cols = pl.ds(pl.multiple_of(ci * 256, 256), 256)
        acc = jnp.dot(xn[0 : 2 * TC, :], we[:, cols], preferred_element_type=F32)
        g = gelu(acc + be[:, cols])
        hid[0, :, cols] = (g[0:TC] * top_ok).astype(BF16)
        hid[TR + 1, :, cols] = (g[TC : 2 * TC] * bot_ok).astype(BF16)
        side = jnp.dot(xcol[...], we[:, cols], preferred_element_type=F32)
        gs = gelu(side + be[:, cols]).astype(BF16).astype(F32)
        ti = lax.broadcasted_iota(jnp.int32, (16, 256), 0)
        edge = jnp.where(ti == 0, top_ok, jnp.where(ti == 9, bot_ok, 1.0))
        gl = gs[0:16] * (edge * left_ok)
        gr = gs[16:32] * (edge * right_ok)
        kl = [dk[a, 0:1, cols] for a in range(3)]
        kr = [dk[a, 2:3, cols] for a in range(3)]
        ledge = gl[0:8] * kl[0] + gl[1:9] * kl[1] + gl[2:10] * kl[2]
        redge = gr[0:8] * kr[0] + gr[1:9] * kr[1] + gr[2:10] * kr[2]
        for i in range(TR):
            hl[i, :, cols] = jnp.broadcast_to(ledge[i : i + 1], (8, 256))
            hr[i, :, cols] = jnp.broadcast_to(redge[i : i + 1], (8, 256))
        return 0

    lax.fori_loop(0, E // 256, halo_chunk, 0)

    bigs[0].wait()
    sub_id = lax.broadcasted_iota(jnp.int32, (8, 128), 0)

    def send_chunk(p):
        return pltpu.make_async_remote_copy(
            src_ref=send.at[p], dst_ref=recv.at[me], send_sem=a_ssem, recv_sem=a_rsem,
            device_id=place(p), device_id_type=MESH,
        )

    def block(k, _):
        b = lax.rem(k + me, 4)

        def lane(ci, _):
            cols = pl.ds(pl.multiple_of(ci * 128, 128), 128)
            rows = [hid[2 * b + i, :, cols].astype(F32) for i in range(4)]
            bias = db[:, cols]
            taps = [[dk[a, q : q + 1, cols] for q in range(3)] for a in range(3)]
            for o in range(2):
                s = [
                    rows[o] * taps[0][q] + rows[o + 1] * taps[1][q] + rows[o + 2] * taps[2][q]
                    for q in range(3)
                ]
                down = pltpu.roll(s[0], 1, 0)
                up = pltpu.roll(s[2], TC - 1, 0)
                first = jnp.where(sub_id == 0, hl[2 * b + o, :, cols], down[0:8])
                last = jnp.where(sub_id == 7, hr[2 * b + o, :, cols], up[TC - 8 : TC])
                total = (
                    s[1] + bias
                    + jnp.concatenate([first, down[8:TC]], axis=0)
                    + jnp.concatenate([up[0 : TC - 8], last], axis=0)
                )
                dwb[o * TC : (o + 1) * TC, cols] = gelu(total).astype(BF16)
            return 0

        lax.fori_loop(0, E // 128, lane, 0)
        proj = jnp.dot(dwb[...], wp[...], preferred_element_type=F32) + bp[...]
        f0 = feat[2 * b].astype(F32)
        f1 = feat[2 * b + 1].astype(F32)
        for o, f in ((0, f0), (1, f1)):
            acb = (f + proj[o * TC : (o + 1) * TC]).astype(BF16)
            feat[2 * b + o] = acb
            wide_ac = acb.astype(F32)
            center = wide_ac - jnp.mean(wide_ac, axis=-1, keepdims=True)
            spread = jnp.mean(center * center, axis=-1, keepdims=True)
            y = (center * lax.rsqrt(spread + 1e-06) * ag[...] + ash[...]).astype(BF16)
            send[pl.ds((2 * b + o) * 8, 8)] = y.reshape(8, 8, C)

        def go(j, _):
            p = 16 * b + lax.rem(j + me, 16)

            @pl.when(p != me)
            def _():
                send_chunk(p).start()

            return 0

        lax.fori_loop(0, 16, go, 0)
        return 0

    lax.fori_loop(0, 4, block, 0)
    accopy = pltpu.make_async_copy(feat, ac_out, out_sem)
    accopy.start()
    recv[pl.ds(me, 1)] = send[pl.ds(me, 1)]
    ri = lax.broadcasted_iota(jnp.int32, (256, 256), 0) // 64
    rj = lax.broadcasted_iota(jnp.int32, (256, 256), 1) // 64
    ones[...] = jnp.where(ri == rj, 1.0, 0.0).astype(BF16)
    bigs[1].wait()
    bigs[2].wait()
    pltpu.make_async_copy(send.at[pl.ds(0, PEERS - 1)], send.at[pl.ds(0, PEERS - 1)], a_ssem).wait()
    pltpu.make_async_copy(recv.at[pl.ds(0, PEERS - 1)], recv.at[pl.ds(0, PEERS - 1)], a_rsem).wait()

    x = recv[...].reshape(TOKENS, C)
    for mb in range(2):
        m = lax.broadcasted_iota(jnp.int32, (256, TOKENS), 0) + mb * 256
        nn = lax.broadcasted_iota(jnp.int32, (256, TOKENS), 1)
        perm = jnp.where(nn == lax.rem(m, 64) * 8 + m // 64, 1.0, 0.0).astype(BF16)
        xp[mb * 256 : (mb + 1) * 256, :] = jnp.dot(perm, x, preferred_element_type=F32).astype(BF16)

    def qkv_chunk(ci, _):
        cols = pl.ds(pl.multiple_of(ci * 256, 256), 256)
        for mb in range(2):
            acc = jnp.dot(
                xp[mb * 256 : (mb + 1) * 256, :], wq[:, cols], preferred_element_type=F32
            )
            qkv[mb * 256 : (mb + 1) * 256, cols] = (acc + bq[:, cols]).astype(BF16)
        return 0

    lax.fori_loop(0, 9, qkv_chunk, 0)

    per = PEERS // NQ
    lane_head = lax.broadcasted_iota(jnp.int32, (64, 128), 1) // HEAD_DIM
    masks = [jnp.where(lane_head == i, 1.0, 0.0).astype(BF16) for i in range(4)]

    def return_chunk(p):
        return pltpu.make_async_remote_copy(
            src_ref=retbuf.at[p], dst_ref=ret_out.at[me], send_sem=b_ssem, recv_sem=b_rsem,
            device_id=place(p), device_id_type=MESH,
        )

    def query_block(qq, _):
        qb = lax.rem(qq + me, NQ)

        def group(g, _):
            krows = pl.ds(pl.multiple_of(g * 64, 64), 64)
            qrows = pl.ds(pl.multiple_of(g * 64 + qb * per, per), per)
            orows = pl.ds(pl.multiple_of(g * per, per), per)
            for quad in range(QUADS):
                lo = quad * 128
                q = qkv[qrows, lo : lo + 128]
                kk = qkv[krows, C + lo : C + lo + 128]
                vv = qkv[krows, 2 * C + lo : 2 * C + lo + 128]
                kbd = jnp.concatenate([kk * m for m in masks], axis=0)
                vbd = jnp.concatenate([vv * m for m in masks], axis=0)
                s = lax.dot_general(
                    q, kbd, (((1,), (1,)), ((), ())), preferred_element_type=F32
                )
                e = jnp.exp2(s * EXP_SCALE)
                tot = jnp.dot(e.astype(BF16), ones[...], preferred_element_type=F32)
                probs = (e / tot).astype(BF16)
                o = jnp.dot(probs, vbd, preferred_element_type=F32)
                mixed[orows, lo : lo + 128] = o.astype(BF16)
            return 0

        lax.fori_loop(0, 8, group, 0)
        rows = per * 8
        m = lax.broadcasted_iota(jnp.int32, (rows, rows), 0)
        nn = lax.broadcasted_iota(jnp.int32, (rows, rows), 1)
        back = jnp.where(nn == lax.rem(m, 8) * per + m // 8, 1.0, 0.0).astype(BF16)
        mm = jnp.dot(back, mixed[...], preferred_element_type=F32).astype(BF16)
        y = (jnp.dot(mm, wo[...], preferred_element_type=F32) + bo[...]).astype(BF16)
        retbuf[pl.ds(qb * per, per)] = y.reshape(per, 8, C)

        def go(j, _):
            p = per * qb + lax.rem(j + me, per)

            @pl.when(p != me)
            def _():
                return_chunk(p).start()

            return 0

        lax.fori_loop(0, per, go, 0)
        return 0

    lax.fori_loop(0, NQ, query_block, 0)
    own = pltpu.make_async_copy(retbuf.at[me], ret_out.at[me], self_sem)
    own.start()
    own.wait()
    accopy.wait()
    pltpu.make_async_copy(retbuf.at[pl.ds(0, PEERS - 1)], retbuf.at[pl.ds(0, PEERS - 1)], b_ssem).wait()
    pltpu.make_async_copy(
        ret_out.at[pl.ds(0, PEERS - 1)], ret_out.at[pl.ds(0, PEERS - 1)], b_rsem
    ).wait()


def per_device(
    features, norm_scale, norm_shift, expand_weight, expand_bias, depth_kernel, depth_bias,
    project_weight, project_bias, attn_gain, attn_shift, qkv_weight, qkv_bias, out_weight, out_bias,
):
    row = lambda v: v.reshape(1, -1)
    args = (
        features, row(norm_scale), row(norm_shift), expand_weight, row(expand_bias), depth_kernel,
        row(depth_bias), project_weight, row(project_bias), row(attn_gain), row(attn_shift),
        qkv_weight, row(qkv_bias), out_weight, row(out_bias),
    )
    vm = pltpu.VMEM
    dma = pltpu.SemaphoreType.DMA
    scratch = [vm(a.shape, a.dtype) for a in args]
    scratch += [
        vm((TOKENS, C), BF16),
        vm((TC, C), BF16),
        vm((TC, C), BF16),
        vm((TR, 8, C), BF16),
        vm((TR, 8, C), BF16),
        vm((4, 8, C), BF16),
        vm((256, C), BF16),
        vm((32, C), BF16),
        vm((TR + 2, TC, E), BF16),
        vm((TR, 8, E), F32),
        vm((TR, 8, E), F32),
        vm((2 * TC, E), BF16),
        vm((PEERS, 8, C), BF16),
        vm((PEERS, 8, C), BF16),
        vm((TOKENS, C), BF16),
        vm((TOKENS, 3 * C), BF16),
        vm((TOKENS // NQ, C), BF16),
        vm((PEERS, 8, C), BF16),
        vm((256, 256), BF16),
        dma((10,)), dma, dma((WCHUNKS,)), dma((3,)), dma((8,)), dma((8,)),
        dma, dma, dma, dma, dma, dma,
    ]
    hbm = pl.BlockSpec(memory_space=pl.ANY)
    after_conv, attended = pl.pallas_call(
        kernel,
        out_shape=(
            jax.ShapeDtypeStruct((TR, TC, C), BF16),
            jax.ShapeDtypeStruct((PEERS, 8, C), BF16),
        ),
        in_specs=[hbm] * len(args),
        out_specs=(hbm, hbm),
        scratch_shapes=scratch,
        name="block",
        compiler_params=pltpu.CompilerParams(
            collective_id=0, has_side_effects=True, vmem_limit_bytes=60 << 20
        ),
    )(*args)
    return (after_conv.astype(F32) + attended.reshape(after_conv.shape).astype(F32)).astype(BF16)


def solution(mesh):
    return jax.shard_map(
        per_device,
        mesh=mesh,
        in_specs=(P("row", "col", None),) + (P(),) * 14,
        out_specs=P("row", "col", None),
        check_vma=False,
    )
```

```python
import math

import jax
import jax.numpy as jnp
from jax import lax
from jax.experimental import pallas as pl
from jax.experimental.pallas import tpu as pltpu
from jax.sharding import PartitionSpec as P

MESH = pl.DeviceIdType.MESH
F32 = jnp.float32
BF16 = jnp.bfloat16

ROWS, COLS = 8, 16
PEERS = 64
TR, TC = 8, 64
TOKENS = TR * TC
C = 768
E = 3072
HEAD_DIM = 32
QUADS = 6
NQ = 2
WCHUNKS = 6
GC1 = math.sqrt(2.0 / math.pi)
GC2 = GC1 * 0.044715
EXP_SCALE = math.log2(math.e) / math.sqrt(HEAD_DIM)


def gelu(v):
    half = 0.5 * v
    return half + half * jnp.tanh(v * (GC1 + GC2 * (v * v)))


def kernel(
    f_hbm, nsc_h, nsh_h, we_h, be_h, dk_h, db_h, wp_h, bp_h, ag_h, as_h, wq_h, bq_h, wo_h, bo_h,
    ac_out, ret_out,
    feat, nsc, nsh, we, be, dk, db, wp, bp, ag, ash, wq, bq, wo, bo,
    xn, top, bot, left, right, corner, xblk, hid, hl, hr, dwb, send, recv, xp, qkv, mixed, retbuf, ones,
    small_sem, feat_sem, we_sem, w_sem, halo_ssem, halo_rsem, a_ssem, a_rsem, b_ssem, b_rsem, out_sem, self_sem,
):
    r = lax.axis_index("row")
    c = lax.axis_index("col")
    core = lax.rem(c, 2)
    me = r * 8 + c // 2

    def place(p):
        return (p // 8, 2 * lax.rem(p, 8) + core)

    bar = pltpu.get_barrier_semaphore()

    fcopy = pltpu.make_async_copy(f_hbm, feat, feat_sem)
    fcopy.start()
    smalls = [
        pltpu.make_async_copy(s, d, small_sem.at[i])
        for i, (s, d) in enumerate(
            ((nsc_h, nsc), (nsh_h, nsh), (be_h, be), (dk_h, dk), (db_h, db), (bp_h, bp),
             (ag_h, ag), (as_h, ash), (bq_h, bq), (bo_h, bo))
        )
    ]
    for s in smalls:
        s.start()
    wide = E // WCHUNKS
    wcopies = [
        pltpu.make_async_copy(
            we_h.at[:, pl.ds(i * wide, wide)], we.at[:, pl.ds(i * wide, wide)], we_sem.at[i]
        )
        for i in range(WCHUNKS)
    ]
    for w in wcopies:
        w.start()

    def signal(i, _):
        pl.semaphore_signal(
            bar, inc=1, device_id=place(lax.rem(me + i, PEERS)), device_id_type=MESH
        )
        return 0

    lax.fori_loop(1, PEERS, signal, 0)
    for dr in (-1, 0, 1):
        for dc in (-1, 1):
            pl.semaphore_signal(
                bar, inc=1,
                device_id=(lax.rem(r + dr + ROWS, ROWS), lax.rem(c + dc + COLS, COLS)),
                device_id_type=MESH,
            )

    bigs = [
        pltpu.make_async_copy(s, d, w_sem.at[i])
        for i, (s, d) in enumerate(((wp_h, wp), (wq_h, wq), (wo_h, wo)))
    ]
    for w in bigs:
        w.start()

    fcopy.wait()
    for s in smalls:
        s.wait()

    def normalise(v):
        return (v.astype(F32) * nsc[...][None, :] + nsh[...][None, :]).astype(BF16)

    def norm_row(h, _):
        xn[pl.ds(pl.multiple_of(h * TC, TC), TC), :] = normalise(feat[h])
        return 0

    lax.fori_loop(0, TR, norm_row, 0)

    def expand_chunk(ci, _):
        cols = pl.ds(pl.multiple_of(ci * 256, 256), 256)
        for mb in range(2):
            acc = jnp.dot(
                xn[mb * 256 : (mb + 1) * 256, :], we[:, cols], preferred_element_type=F32
            )
            g = gelu(acc + be[:, cols]).astype(BF16)
            hid[1 + 4 * mb : 5 + 4 * mb, :, cols] = g.reshape(4, TC, 256)
        return 0

    early = 4
    for i in range(early):
        wcopies[i].wait()
        lax.fori_loop(2 * i, 2 * i + 2, expand_chunk, 0)

    pl.semaphore_wait(bar, PEERS - 1 + 6)

    def halo(src, dst, k, dr, dc):
        return pltpu.make_async_remote_copy(
            src_ref=src, dst_ref=dst, send_sem=halo_ssem.at[k], recv_sem=halo_rsem.at[k],
            device_id=(lax.rem(r + dr + ROWS, ROWS), lax.rem(c + dc + COLS, COLS)),
            device_id_type=MESH,
        )

    halos = [
        halo(feat.at[TR - 1], top, 0, 1, 0),
        halo(feat.at[0], bot, 1, -1, 0),
        halo(feat.at[:, pl.ds(TC - 8, 8)], left, 2, 0, 1),
        halo(feat.at[:, pl.ds(0, 8)], right, 3, 0, -1),
        halo(feat.at[TR - 1, pl.ds(TC - 8, 8)], corner.at[0], 4, 1, 1),
        halo(feat.at[0, pl.ds(TC - 8, 8)], corner.at[1], 5, -1, 1),
        halo(feat.at[TR - 1, pl.ds(0, 8)], corner.at[2], 6, 1, -1),
        halo(feat.at[0, pl.ds(0, 8)], corner.at[3], 7, -1, -1),
    ]
    for h in halos:
        h.start()

    for i in range(early, WCHUNKS):
        wcopies[i].wait()
        lax.fori_loop(2 * i, 2 * i + 2, expand_chunk, 0)

    for h in halos:
        h.wait()

    top_ok = jnp.where(r > 0, 1.0, 0.0).astype(F32)
    bot_ok = jnp.where(r < ROWS - 1, 1.0, 0.0).astype(F32)
    left_ok = jnp.where(c > 0, 1.0, 0.0).astype(F32)
    right_ok = jnp.where(c < COLS - 1, 1.0, 0.0).astype(F32)

    xn[0:TC, :] = normalise(top[...])
    xn[TC : 2 * TC, :] = normalise(bot[...])
    for i in range(TR):
        xblk[i * 8 : i * 8 + 8, :] = normalise(left[i])
        xblk[64 + i * 8 : 64 + i * 8 + 8, :] = normalise(right[i])
    for i in range(4):
        xblk[128 + i * 8 : 136 + i * 8, :] = normalise(corner[i])
    xblk[160:256, :] = jnp.zeros((96, C), BF16)
    t = lax.broadcasted_iota(jnp.int32, (32, 256), 0)
    n = lax.broadcasted_iota(jnp.int32, (32, 256), 1)
    tr = lax.rem(t, 16)
    want_l = jnp.where(tr == 0, 135, jnp.where(tr == 9, 143, (tr - 1) * 8 + 7))
    want_r = jnp.where(tr == 0, 144, jnp.where(tr == 9, 152, 64 + (tr - 1) * 8))
    want = jnp.where(t < 16, want_l, want_r)
    want = jnp.where(tr <= 9, want, -1)
    pick = jnp.where(n == want, 1.0, 0.0).astype(BF16)
    xn[2 * TC : 2 * TC + 32, :] = jnp.dot(
        pick, xblk[...], preferred_element_type=F32
    ).astype(BF16)

    def halo_chunk(ci, _):
        cols = pl.ds(pl.multiple_of(ci * 256, 256), 256)
        acc = jnp.dot(xn[0 : 2 * TC + 32, :], we[:, cols], preferred_element_type=F32)
        g = gelu(acc + be[:, cols])
        hid[0, :, cols] = (g[0:TC] * top_ok).astype(BF16)
        hid[TR + 1, :, cols] = (g[TC : 2 * TC] * bot_ok).astype(BF16)
        gs = g[2 * TC : 2 * TC + 32].astype(BF16).astype(F32)
        ti = lax.broadcasted_iota(jnp.int32, (16, 256), 0)
        edge = jnp.where(ti == 0, top_ok, jnp.where(ti == 9, bot_ok, 1.0))
        gl = gs[0:16] * (edge * left_ok)
        gr = gs[16:32] * (edge * right_ok)
        kl = [dk[a, 0:1, cols] for a in range(3)]
        kr = [dk[a, 2:3, cols] for a in range(3)]
        ledge = gl[0:8] * kl[0] + gl[1:9] * kl[1] + gl[2:10] * kl[2]
        redge = gr[0:8] * kr[0] + gr[1:9] * kr[1] + gr[2:10] * kr[2]
        for i in range(TR):
            hl[i, :, cols] = jnp.broadcast_to(ledge[i : i + 1], (8, 256))
            hr[i, :, cols] = jnp.broadcast_to(redge[i : i + 1], (8, 256))
        return 0

    lax.fori_loop(0, E // 256, halo_chunk, 0)

    bigs[0].wait()
    sub_id = lax.broadcasted_iota(jnp.int32, (8, 128), 0)

    def send_chunk(p):
        return pltpu.make_async_remote_copy(
            src_ref=send.at[p], dst_ref=recv.at[me], send_sem=a_ssem, recv_sem=a_rsem,
            device_id=place(p), device_id_type=MESH,
        )

    def block(k, _):
        b = lax.rem(k + me, 4)

        def lane(ci, _):
            cols = pl.ds(pl.multiple_of(ci * 128, 128), 128)
            rows = [hid[2 * b + i, :, cols].astype(F32) for i in range(4)]
            bias = db[:, cols]
            taps = [[dk[a, q : q + 1, cols] for q in range(3)] for a in range(3)]
            for o in range(2):
                s = [
                    rows[o] * taps[0][q] + rows[o + 1] * taps[1][q] + rows[o + 2] * taps[2][q]
                    for q in range(3)
                ]
                down = pltpu.roll(s[0], 1, 0)
                up = pltpu.roll(s[2], TC - 1, 0)
                first = jnp.where(sub_id == 0, hl[2 * b + o, :, cols], down[0:8])
                last = jnp.where(sub_id == 7, hr[2 * b + o, :, cols], up[TC - 8 : TC])
                total = (
                    s[1] + bias
                    + jnp.concatenate([first, down[8:TC]], axis=0)
                    + jnp.concatenate([up[0 : TC - 8], last], axis=0)
                )
                dwb[o * TC : (o + 1) * TC, cols] = gelu(total).astype(BF16)
            return 0

        lax.fori_loop(0, E // 128, lane, 0)
        proj = jnp.dot(dwb[...], wp[...], preferred_element_type=F32) + bp[...][None, :]
        f0 = feat[2 * b].astype(F32)
        f1 = feat[2 * b + 1].astype(F32)
        for o, f in ((0, f0), (1, f1)):
            acb = (f + proj[o * TC : (o + 1) * TC]).astype(BF16)
            feat[2 * b + o] = acb
            wide_ac = acb.astype(F32)
            center = wide_ac - jnp.mean(wide_ac, axis=-1, keepdims=True)
            spread = jnp.mean(center * center, axis=-1, keepdims=True)
            y = (center * lax.rsqrt(spread + 1e-06) * ag[...][None, :] + ash[...][None, :]).astype(BF16)
            send[pl.ds((2 * b + o) * 8, 8)] = y.reshape(8, 8, C)

        def go(j, _):
            p = 16 * b + lax.rem(j + me, 16)

            @pl.when(p != me)
            def _():
                send_chunk(p).start()

            return 0

        lax.fori_loop(0, 16, go, 0)
        return 0

    lax.fori_loop(0, 4, block, 0)
    accopy = pltpu.make_async_copy(feat, ac_out, out_sem)
    accopy.start()
    recv[pl.ds(me, 1)] = send[pl.ds(me, 1)]
    ri = lax.broadcasted_iota(jnp.int32, (256, 256), 0) // 64
    rj = lax.broadcasted_iota(jnp.int32, (256, 256), 1) // 64
    ones[...] = jnp.where(ri == rj, 1.0, 0.0).astype(BF16)
    bigs[1].wait()
    bigs[2].wait()
    pltpu.make_async_copy(send.at[pl.ds(0, PEERS - 1)], send.at[pl.ds(0, PEERS - 1)], a_ssem).wait()
    pltpu.make_async_copy(recv.at[pl.ds(0, PEERS - 1)], recv.at[pl.ds(0, PEERS - 1)], a_rsem).wait()

    x = recv[...].reshape(TOKENS, C)
    for mb in range(2):
        m = lax.broadcasted_iota(jnp.int32, (256, TOKENS), 0) + mb * 256
        nn = lax.broadcasted_iota(jnp.int32, (256, TOKENS), 1)
        perm = jnp.where(nn == lax.rem(m, 64) * 8 + m // 64, 1.0, 0.0).astype(BF16)
        xp[mb * 256 : (mb + 1) * 256, :] = jnp.dot(perm, x, preferred_element_type=F32).astype(BF16)

    def qkv_chunk(ci, _):
        cols = pl.ds(pl.multiple_of(ci * 256, 256), 256)
        for mb in range(2):
            acc = jnp.dot(
                xp[mb * 256 : (mb + 1) * 256, :], wq[:, cols], preferred_element_type=F32
            )
            qkv[mb * 256 : (mb + 1) * 256, cols] = (acc + bq[cols][None, :]).astype(BF16)
        return 0

    lax.fori_loop(0, 9, qkv_chunk, 0)

    per = PEERS // NQ
    lane_head = lax.broadcasted_iota(jnp.int32, (64, 128), 1) // HEAD_DIM
    masks = [jnp.where(lane_head == i, 1.0, 0.0).astype(BF16) for i in range(4)]

    def return_chunk(p):
        return pltpu.make_async_remote_copy(
            src_ref=retbuf.at[p], dst_ref=ret_out.at[me], send_sem=b_ssem, recv_sem=b_rsem,
            device_id=place(p), device_id_type=MESH,
        )

    def query_block(qq, _):
        qb = lax.rem(qq + me, NQ)

        def group(g, _):
            krows = pl.ds(pl.multiple_of(g * 64, 64), 64)
            qrows = pl.ds(pl.multiple_of(g * 64 + qb * per, per), per)
            orows = pl.ds(pl.multiple_of(g * per, per), per)
            es = []
            for quad in range(QUADS):
                lo = quad * 128
                q = qkv[qrows, lo : lo + 128]
                kk = qkv[krows, C + lo : C + lo + 128]
                kbd = jnp.concatenate([kk * m for m in masks], axis=0)
                s = lax.dot_general(
                    q, kbd, (((1,), (1,)), ((), ())), preferred_element_type=F32
                )
                es.append(jnp.exp2(s * EXP_SCALE))
            e = jnp.concatenate(es, axis=0)
            tot = jnp.dot(e.astype(BF16), ones[...], preferred_element_type=F32)
            probs = (e / tot).astype(BF16)
            for quad in range(QUADS):
                lo = quad * 128
                vv = qkv[krows, 2 * C + lo : 2 * C + lo + 128]
                vbd = jnp.concatenate([vv * m for m in masks], axis=0)
                o = jnp.dot(
                    probs[quad * per : (quad + 1) * per], vbd, preferred_element_type=F32
                )
                mixed[orows, lo : lo + 128] = o.astype(BF16)
            return 0

        lax.fori_loop(0, 8, group, 0)
        rows = per * 8
        m = lax.broadcasted_iota(jnp.int32, (rows, rows), 0)
        nn = lax.broadcasted_iota(jnp.int32, (rows, rows), 1)
        back = jnp.where(nn == lax.rem(m, 8) * per + m // 8, 1.0, 0.0).astype(BF16)
        mm = jnp.dot(back, mixed[...], preferred_element_type=F32).astype(BF16)
        y = (jnp.dot(mm, wo[...], preferred_element_type=F32) + bo[...][None, :]).astype(BF16)
        retbuf[pl.ds(qb * per, per)] = y.reshape(per, 8, C)

        def go(j, _):
            p = per * qb + lax.rem(j + me, per)

            @pl.when(p != me)
            def _():
                return_chunk(p).start()

            return 0

        lax.fori_loop(0, per, go, 0)
        return 0

    lax.fori_loop(0, NQ, query_block, 0)
    own = pltpu.make_async_copy(retbuf.at[me], ret_out.at[me], self_sem)
    own.start()
    own.wait()
    accopy.wait()
    pltpu.make_async_copy(retbuf.at[pl.ds(0, PEERS - 1)], retbuf.at[pl.ds(0, PEERS - 1)], b_ssem).wait()
    pltpu.make_async_copy(
        ret_out.at[pl.ds(0, PEERS - 1)], ret_out.at[pl.ds(0, PEERS - 1)], b_rsem
    ).wait()


def per_device(
    features, norm_scale, norm_shift, expand_weight, expand_bias, depth_kernel, depth_bias,
    project_weight, project_bias, attn_gain, attn_shift, qkv_weight, qkv_bias, out_weight, out_bias,
):
    row = lambda v: v if v.shape[0] % 1024 else v.reshape(1, -1)
    args = (
        features, row(norm_scale), row(norm_shift), expand_weight, row(expand_bias), depth_kernel,
        row(depth_bias), project_weight, row(project_bias), row(attn_gain), row(attn_shift),
        qkv_weight, row(qkv_bias), out_weight, row(out_bias),
    )
    vm = pltpu.VMEM
    dma = pltpu.SemaphoreType.DMA
    scratch = [vm(a.shape, a.dtype) for a in args]
    scratch += [
        vm((TOKENS, C), BF16),
        vm((TC, C), BF16),
        vm((TC, C), BF16),
        vm((TR, 8, C), BF16),
        vm((TR, 8, C), BF16),
        vm((4, 8, C), BF16),
        vm((256, C), BF16),
        vm((TR + 2, TC, E), BF16),
        vm((TR, 8, E), F32),
        vm((TR, 8, E), F32),
        vm((2 * TC, E), BF16),
        vm((PEERS, 8, C), BF16),
        vm((PEERS, 8, C), BF16),
        vm((TOKENS, C), BF16),
        vm((TOKENS, 3 * C), BF16),
        vm((TOKENS // NQ, C), BF16),
        vm((PEERS, 8, C), BF16),
        vm((256, 256), BF16),
        dma((10,)), dma, dma((WCHUNKS,)), dma((3,)), dma((8,)), dma((8,)),
        dma, dma, dma, dma, dma, dma,
    ]
    hbm = pl.BlockSpec(memory_space=pl.ANY)
    after_conv, attended = pl.pallas_call(
        kernel,
        out_shape=(
            jax.ShapeDtypeStruct((TR, TC, C), BF16),
            jax.ShapeDtypeStruct((PEERS, 8, C), BF16),
        ),
        in_specs=[hbm] * len(args),
        out_specs=(hbm, hbm),
        scratch_shapes=scratch,
        name="block",
        compiler_params=pltpu.CompilerParams(
            collective_id=0, has_side_effects=True, vmem_limit_bytes=60 << 20
        ),
    )(*args)
    return (after_conv.astype(F32) + attended.reshape(after_conv.shape).astype(F32)).astype(BF16)


def solution(mesh):
    return jax.shard_map(
        per_device,
        mesh=mesh,
        in_specs=(P("row", "col", None),) + (P(),) * 14,
        out_specs=P("row", "col", None),
        check_vma=False,
    )
```

```python
import math

import jax
import jax.numpy as jnp
from jax import lax
from jax.experimental import pallas as pl
from jax.experimental.pallas import tpu as pltpu
from jax.sharding import PartitionSpec as P

MESH = pl.DeviceIdType.MESH
F32 = jnp.float32
BF16 = jnp.bfloat16

ROWS, COLS = 8, 16
PEERS = 64
TR, TC = 8, 64
TOKENS = TR * TC
C = 768
E = 3072
HEAD_DIM = 32
QUADS = 6
NSUB = 2
PER = 8 // NSUB
PER_BITS = PER.bit_length() - 1
WCHUNKS = 6
GC1 = math.sqrt(2.0 / math.pi)
GC2 = GC1 * 0.044715
EXP_SCALE = math.log2(math.e) / math.sqrt(HEAD_DIM)


def gelu(v):
    half = 0.5 * v
    return half + half * jnp.tanh(v * (GC1 + GC2 * (v * v)))


def kernel(
    f_hbm, nsc_h, nsh_h, we_h, be_h, dk_h, db_h, wp_h, bp_h, ag_h, as_h, wq_h, bq_h, wo_h, bo_h,
    ac_out, ret_out,
    feat, nsc, nsh, we, be, dk, db, wp, bp, ag, ash, wq, bq, wo, bo,
    xn, top, bot, left, right, corner, xblk, hid, hl, hr, dwb, send, recv, xp, qkv, mixed, retbuf, acc, ones,
    small_sem, feat_sem, we_sem, w_sem, halo_ssem, halo_rsem, a_ssem, a_rsem, b_ssem, b_rsem, out_sem, self_sem,
):
    r = lax.axis_index("row")
    c = lax.axis_index("col")
    core = lax.rem(c, 2)
    me = r * 8 + c // 2

    def place(p):
        return (p // 8, 2 * lax.rem(p, 8) + core)

    bar = pltpu.get_barrier_semaphore()

    fcopy = pltpu.make_async_copy(f_hbm, feat, feat_sem)
    fcopy.start()
    smalls = [
        pltpu.make_async_copy(s, d, small_sem.at[i])
        for i, (s, d) in enumerate(
            ((nsc_h, nsc), (nsh_h, nsh), (be_h, be), (dk_h, dk), (db_h, db), (bp_h, bp),
             (ag_h, ag), (as_h, ash), (bq_h, bq), (bo_h, bo))
        )
    ]
    for s in smalls:
        s.start()
    wide = E // WCHUNKS
    wcopies = [
        pltpu.make_async_copy(
            we_h.at[:, pl.ds(i * wide, wide)], we.at[:, pl.ds(i * wide, wide)], we_sem.at[i]
        )
        for i in range(WCHUNKS)
    ]
    for w in wcopies:
        w.start()

    def signal(i, _):
        pl.semaphore_signal(
            bar, inc=1, device_id=place(lax.rem(me + i, PEERS)), device_id_type=MESH
        )
        return 0

    lax.fori_loop(1, PEERS, signal, 0)
    for dr in (-1, 0, 1):
        for dc in (-1, 1):
            pl.semaphore_signal(
                bar, inc=1,
                device_id=(lax.rem(r + dr + ROWS, ROWS), lax.rem(c + dc + COLS, COLS)),
                device_id_type=MESH,
            )

    bigs = [
        pltpu.make_async_copy(s, d, w_sem.at[i])
        for i, (s, d) in enumerate(((wp_h, wp), (wq_h, wq), (wo_h, wo)))
    ]
    for w in bigs:
        w.start()

    fcopy.wait()
    for s in smalls:
        s.wait()

    def normalise(v):
        return (v.astype(F32) * nsc[...][None, :] + nsh[...][None, :]).astype(BF16)

    def norm_row(h, _):
        xn[pl.ds(pl.multiple_of(h * TC, TC), TC), :] = normalise(feat[h])
        return 0

    lax.fori_loop(0, TR, norm_row, 0)

    def expand_chunk(ci, _):
        cols = pl.ds(pl.multiple_of(ci * 256, 256), 256)
        for mb in range(2):
            acc = jnp.dot(
                xn[mb * 256 : (mb + 1) * 256, :], we[:, cols], preferred_element_type=F32
            )
            g = gelu(acc + be[:, cols]).astype(BF16)
            hid[1 + 4 * mb : 5 + 4 * mb, :, cols] = g.reshape(4, TC, 256)
        return 0

    early = 4
    for i in range(early):
        wcopies[i].wait()
        lax.fori_loop(2 * i, 2 * i + 2, expand_chunk, 0)

    pl.semaphore_wait(bar, PEERS - 1 + 6)

    def halo(src, dst, k, dr, dc):
        return pltpu.make_async_remote_copy(
            src_ref=src, dst_ref=dst, send_sem=halo_ssem.at[k], recv_sem=halo_rsem.at[k],
            device_id=(lax.rem(r + dr + ROWS, ROWS), lax.rem(c + dc + COLS, COLS)),
            device_id_type=MESH,
        )

    halos = [
        halo(feat.at[TR - 1], top, 0, 1, 0),
        halo(feat.at[0], bot, 1, -1, 0),
        halo(feat.at[:, pl.ds(TC - 8, 8)], left, 2, 0, 1),
        halo(feat.at[:, pl.ds(0, 8)], right, 3, 0, -1),
        halo(feat.at[TR - 1, pl.ds(TC - 8, 8)], corner.at[0], 4, 1, 1),
        halo(feat.at[0, pl.ds(TC - 8, 8)], corner.at[1], 5, -1, 1),
        halo(feat.at[TR - 1, pl.ds(0, 8)], corner.at[2], 6, 1, -1),
        halo(feat.at[0, pl.ds(0, 8)], corner.at[3], 7, -1, -1),
    ]
    for h in halos:
        h.start()

    for i in range(early, WCHUNKS):
        wcopies[i].wait()
        lax.fori_loop(2 * i, 2 * i + 2, expand_chunk, 0)

    for h in halos:
        h.wait()

    top_ok = jnp.where(r > 0, 1.0, 0.0).astype(F32)
    bot_ok = jnp.where(r < ROWS - 1, 1.0, 0.0).astype(F32)
    left_ok = jnp.where(c > 0, 1.0, 0.0).astype(F32)
    right_ok = jnp.where(c < COLS - 1, 1.0, 0.0).astype(F32)

    xn[0:TC, :] = normalise(top[...])
    xn[TC : 2 * TC, :] = normalise(bot[...])
    for i in range(TR):
        xblk[i * 8 : i * 8 + 8, :] = normalise(left[i])
        xblk[64 + i * 8 : 64 + i * 8 + 8, :] = normalise(right[i])
    for i in range(4):
        xblk[128 + i * 8 : 136 + i * 8, :] = normalise(corner[i])
    xblk[160:256, :] = jnp.zeros((96, C), BF16)
    t = lax.broadcasted_iota(jnp.int32, (32, 256), 0)
    n = lax.broadcasted_iota(jnp.int32, (32, 256), 1)
    tr = lax.rem(t, 16)
    want_l = jnp.where(tr == 0, 135, jnp.where(tr == 9, 143, (tr - 1) * 8 + 7))
    want_r = jnp.where(tr == 0, 144, jnp.where(tr == 9, 152, 64 + (tr - 1) * 8))
    want = jnp.where(t < 16, want_l, want_r)
    want = jnp.where(tr <= 9, want, -1)
    pick = jnp.where(n == want, 1.0, 0.0).astype(BF16)
    xn[2 * TC : 2 * TC + 32, :] = jnp.dot(
        pick, xblk[...], preferred_element_type=F32
    ).astype(BF16)

    def halo_chunk(ci, _):
        cols = pl.ds(pl.multiple_of(ci * 256, 256), 256)
        acc = jnp.dot(xn[0 : 2 * TC + 32, :], we[:, cols], preferred_element_type=F32)
        g = gelu(acc + be[:, cols])
        hid[0, :, cols] = (g[0:TC] * top_ok).astype(BF16)
        hid[TR + 1, :, cols] = (g[TC : 2 * TC] * bot_ok).astype(BF16)
        gs = g[2 * TC : 2 * TC + 32].astype(BF16).astype(F32)
        ti = lax.broadcasted_iota(jnp.int32, (16, 256), 0)
        edge = jnp.where(ti == 0, top_ok, jnp.where(ti == 9, bot_ok, 1.0))
        gl = gs[0:16] * (edge * left_ok)
        gr = gs[16:32] * (edge * right_ok)
        kl = [dk[a, 0:1, cols] for a in range(3)]
        kr = [dk[a, 2:3, cols] for a in range(3)]
        ledge = gl[0:8] * kl[0] + gl[1:9] * kl[1] + gl[2:10] * kl[2]
        redge = gr[0:8] * kr[0] + gr[1:9] * kr[1] + gr[2:10] * kr[2]
        for i in range(TR):
            hl[i, :, cols] = jnp.broadcast_to(ledge[i : i + 1], (8, 256))
            hr[i, :, cols] = jnp.broadcast_to(redge[i : i + 1], (8, 256))
        return 0

    lax.fori_loop(0, E // 256, halo_chunk, 0)

    bigs[0].wait()
    sub_id = lax.broadcasted_iota(jnp.int32, (8, 128), 0)

    def send_chunk(p):
        return pltpu.make_async_remote_copy(
            src_ref=send.at[p], dst_ref=recv.at[me], send_sem=a_ssem, recv_sem=a_rsem,
            device_id=place(p), device_id_type=MESH,
        )

    def block(k, _):
        b = lax.rem(k + me, 4)

        def depthwise(ci):
            for half in range(2):
                cols = pl.ds(pl.multiple_of(ci * 256 + half * 128, 128), 128)
                rows = [hid[2 * b + i, :, cols].astype(F32) for i in range(4)]
                bias = db[:, cols]
                taps = [[dk[a, q : q + 1, cols] for q in range(3)] for a in range(3)]
                for o in range(2):
                    s = [
                        rows[o] * taps[0][q] + rows[o + 1] * taps[1][q] + rows[o + 2] * taps[2][q]
                        for q in range(3)
                    ]
                    down = pltpu.roll(s[0], 1, 0)
                    up = pltpu.roll(s[2], TC - 1, 0)
                    first = jnp.where(sub_id == 0, hl[2 * b + o, :, cols], down[0:8])
                    last = jnp.where(sub_id == 7, hr[2 * b + o, :, cols], up[TC - 8 : TC])
                    total = (
                        s[1] + bias
                        + jnp.concatenate([first, down[8:TC]], axis=0)
                        + jnp.concatenate([up[0 : TC - 8], last], axis=0)
                    )
                    dwb[o * TC : (o + 1) * TC, cols] = gelu(total).astype(BF16)

        def project(ci):
            part = pl.ds(pl.multiple_of(ci * 256, 256), 256)
            acc[...] += jnp.dot(dwb[:, part], wp[part, :], preferred_element_type=F32)

        def lane(ci, _):
            project(ci - 1)
            depthwise(ci)
            return 0

        acc[...] = jnp.broadcast_to(bp[...][None, :], (2 * TC, C))
        depthwise(0)
        lax.fori_loop(1, E // 256, lane, 0)
        project(E // 256 - 1)
        proj = acc[...]
        f0 = feat[2 * b].astype(F32)
        f1 = feat[2 * b + 1].astype(F32)
        for o, f in ((0, f0), (1, f1)):
            acb = (f + proj[o * TC : (o + 1) * TC]).astype(BF16)
            feat[2 * b + o] = acb
            wide_ac = acb.astype(F32)
            center = wide_ac - jnp.mean(wide_ac, axis=-1, keepdims=True)
            spread = jnp.mean(center * center, axis=-1, keepdims=True)
            y = (center * lax.rsqrt(spread + 1e-06) * ag[...][None, :] + ash[...][None, :]).astype(BF16)
            send[pl.ds((2 * b + o) * 8, 8)] = y.reshape(8, 8, C)

        def go(j, _):
            p = 16 * b + lax.rem(j + me, 16)

            @pl.when(p != me)
            def _():
                send_chunk(p).start()

            return 0

        lax.fori_loop(0, 16, go, 0)
        return 0

    lax.fori_loop(0, 4, block, 0)
    accopy = pltpu.make_async_copy(feat, ac_out, out_sem)
    accopy.start()
    recv[pl.ds(me, 1)] = send[pl.ds(me, 1)]
    ri = lax.broadcasted_iota(jnp.int32, (256, 256), 0) >> 6
    rj = lax.broadcasted_iota(jnp.int32, (256, 256), 1) >> 6
    ones[...] = jnp.where(ri == rj, 1.0, 0.0).astype(BF16)
    bigs[1].wait()
    bigs[2].wait()
    pltpu.make_async_copy(send.at[pl.ds(0, PEERS - 1)], send.at[pl.ds(0, PEERS - 1)], a_ssem).wait()
    pltpu.make_async_copy(recv.at[pl.ds(0, PEERS - 1)], recv.at[pl.ds(0, PEERS - 1)], a_rsem).wait()

    lane_head = lax.broadcasted_iota(jnp.int32, (64, 128), 1) >> 5
    masks = [jnp.where(lane_head == i, 1.0, 0.0).astype(BF16) for i in range(4)]

    def return_chunk(p, sub):
        return pltpu.make_async_remote_copy(
            src_ref=retbuf.at[sub, p], dst_ref=ret_out.at[me, pl.ds(PER * sub, PER)],
            send_sem=b_ssem, recv_sem=b_rsem, device_id=place(p), device_id_type=MESH,
        )

    subrows = PER * PEERS

    for sub in range(NSUB):
        m = lax.broadcasted_iota(jnp.int32, (subrows, TOKENS), 0)
        nn = lax.broadcasted_iota(jnp.int32, (subrows, TOKENS), 1)
        perm = jnp.where(nn == (m & 63) * 8 + (m >> 6) + PER * sub, 1.0, 0.0).astype(BF16)
        xp[...] = jnp.dot(
            perm, recv[...].reshape(TOKENS, C), preferred_element_type=F32
        ).astype(BF16)

        def qkv_chunk(ci, _):
            cols = pl.ds(pl.multiple_of(ci * 256, 256), 256)
            part = jnp.dot(xp[...], wq[:, cols], preferred_element_type=F32)
            qkv[:, cols] = (part + bq[cols][None, :]).astype(BF16)
            return 0

        lax.fori_loop(0, 9, qkv_chunk, 0)

        def group(g, _):
            rows = pl.ds(pl.multiple_of(g * 64, 64), 64)
            es = []
            for quad in range(QUADS):
                lo = quad * 128
                q = qkv[rows, lo : lo + 128]
                kk = qkv[rows, C + lo : C + lo + 128]
                kbd = jnp.concatenate([kk * m for m in masks], axis=0)
                s = lax.dot_general(
                    q, kbd, (((1,), (1,)), ((), ())), preferred_element_type=F32
                )
                es.append(jnp.exp2(s * EXP_SCALE))
            e = jnp.concatenate(es, axis=0)
            tot = jnp.dot(e.astype(BF16), ones[...], preferred_element_type=F32)
            probs = (e / tot).astype(BF16)
            for quad in range(QUADS):
                lo = quad * 128
                vv = qkv[rows, 2 * C + lo : 2 * C + lo + 128]
                vbd = jnp.concatenate([vv * m for m in masks], axis=0)
                o = jnp.dot(
                    probs[quad * 64 : (quad + 1) * 64], vbd, preferred_element_type=F32
                )
                mixed[rows, lo : lo + 128] = o.astype(BF16)
            return 0

        lax.fori_loop(0, PER, group, 0)
        m = lax.broadcasted_iota(jnp.int32, (subrows, subrows), 0)
        nn = lax.broadcasted_iota(jnp.int32, (subrows, subrows), 1)
        back = jnp.where(
            nn == (m & (PER - 1)) * 64 + (m >> PER_BITS), 1.0, 0.0
        ).astype(BF16)
        mm = jnp.dot(back, mixed[...], preferred_element_type=F32).astype(BF16)
        y = (jnp.dot(mm, wo[...], preferred_element_type=F32) + bo[...][None, :]).astype(BF16)
        retbuf[sub] = y.reshape(PEERS, PER, C)
        pltpu.make_async_copy(
            retbuf.at[sub, me], ret_out.at[me, pl.ds(PER * sub, PER)], self_sem.at[sub]
        ).start()

        def go(j, _):
            return_chunk(lax.rem(j + me, PEERS), sub).start()
            return 0

        lax.fori_loop(1, PEERS, go, 0)

    for sub in range(NSUB):
        pltpu.make_async_copy(
            retbuf.at[sub, me], ret_out.at[me, pl.ds(PER * sub, PER)], self_sem.at[sub]
        ).wait()
    accopy.wait()
    pltpu.make_async_copy(ret_out.at[pl.ds(0, PEERS - 1)], ret_out.at[pl.ds(0, PEERS - 1)], b_ssem).wait()
    pltpu.make_async_copy(ret_out.at[pl.ds(0, PEERS - 1)], ret_out.at[pl.ds(0, PEERS - 1)], b_rsem).wait()


def per_device(
    features, norm_scale, norm_shift, expand_weight, expand_bias, depth_kernel, depth_bias,
    project_weight, project_bias, attn_gain, attn_shift, qkv_weight, qkv_bias, out_weight, out_bias,
):
    row = lambda v: v if v.shape[0] % 1024 else v.reshape(1, -1)
    args = (
        features, row(norm_scale), row(norm_shift), expand_weight, row(expand_bias), depth_kernel,
        row(depth_bias), project_weight, row(project_bias), row(attn_gain), row(attn_shift),
        qkv_weight, row(qkv_bias), out_weight, row(out_bias),
    )
    vm = pltpu.VMEM
    dma = pltpu.SemaphoreType.DMA
    scratch = [vm(a.shape, a.dtype) for a in args]
    scratch += [
        vm((TOKENS, C), BF16),
        vm((TC, C), BF16),
        vm((TC, C), BF16),
        vm((TR, 8, C), BF16),
        vm((TR, 8, C), BF16),
        vm((4, 8, C), BF16),
        vm((256, C), BF16),
        vm((TR + 2, TC, E), BF16),
        vm((TR, 8, E), F32),
        vm((TR, 8, E), F32),
        vm((2 * TC, E), BF16),
        vm((PEERS, 8, C), BF16),
        vm((PEERS, 8, C), BF16),
        vm((TOKENS // NSUB, C), BF16),
        vm((TOKENS // NSUB, 3 * C), BF16),
        vm((TOKENS // NSUB, C), BF16),
        vm((NSUB, PEERS, PER, C), BF16),
        vm((2 * TC, C), F32),
        vm((256, 256), BF16),
        dma((10,)), dma, dma((WCHUNKS,)), dma((3,)), dma((8,)), dma((8,)),
        dma, dma, dma, dma, dma, dma((NSUB,)),
    ]
    hbm = pl.BlockSpec(memory_space=pl.ANY)
    after_conv, attended = pl.pallas_call(
        kernel,
        out_shape=(
            jax.ShapeDtypeStruct((TR, TC, C), BF16),
            jax.ShapeDtypeStruct((PEERS, 8, C), BF16),
        ),
        in_specs=[hbm] * len(args),
        out_specs=(hbm, hbm),
        scratch_shapes=scratch,
        name="block",
        compiler_params=pltpu.CompilerParams(
            collective_id=0, has_side_effects=True, vmem_limit_bytes=60 << 20
        ),
    )(*args)
    return (after_conv.astype(F32) + attended.reshape(after_conv.shape).astype(F32)).astype(BF16)


def solution(mesh):
    return jax.shard_map(
        per_device,
        mesh=mesh,
        in_specs=(P("row", "col", None),) + (P(),) * 14,
        out_specs=P("row", "col", None),
        check_vma=False,
    )
```

```python
import math

import jax
import jax.numpy as jnp
from jax import lax
from jax.experimental import pallas as pl
from jax.experimental.pallas import tpu as pltpu
from jax.sharding import PartitionSpec as P

MESH = pl.DeviceIdType.MESH
F32 = jnp.float32
BF16 = jnp.bfloat16

ROWS, COLS = 8, 16
PEERS = 64
TR, TC = 8, 64
TOKENS = TR * TC
C = 768
E = 3072
HEAD_DIM = 32
QUADS = 6
NSUB = 2
PER = 8 // NSUB
PER_BITS = PER.bit_length() - 1
WCHUNKS = 6
GC1 = math.sqrt(2.0 / math.pi)
GC2 = GC1 * 0.044715
EXP_SCALE = math.log2(math.e) / math.sqrt(HEAD_DIM)


def gelu(v):
    half = 0.5 * v
    return half + half * jnp.tanh(v * (GC1 + GC2 * (v * v)))


def kernel(
    f_hbm, nsc_h, nsh_h, we_h, be_h, dk_h, db_h, wp_h, bp_h, ag_h, as_h, wq_h, bq_h, wo_h, bo_h,
    ac_out, ret_out,
    feat, nsc, nsh, we, be, dk, db, wp, bp, ag, ash, wq, bq, wo, bo,
    xn, top, bot, left, right, corner, xblk, hid, hl, hr, dwb, send, recv, xp, qkv, mixed, retbuf, acc, ones,
    small_sem, feat_sem, we_sem, w_sem, halo_ssem, halo_rsem, a_ssem, a_rsem, b_ssem, b_rsem, out_sem, self_sem,
):
    r = lax.axis_index("row")
    c = lax.axis_index("col")
    core = c & 1
    x, y, z = r & 3, ((r >> 2) << 1) + ((c >> 1) & 1), c >> 2
    me = (((x + y + z) & 3) << 4) + (y << 2) + z

    def place(k):
        y, z = (k >> 2) & 3, k & 3
        x = ((k >> 4) - y - z) & 3
        return (((y >> 1) << 2) + x, (z << 2) + ((y & 1) << 1) + core)

    bar = pltpu.get_barrier_semaphore()

    fcopy = pltpu.make_async_copy(f_hbm, feat, feat_sem)
    fcopy.start()
    smalls = [
        pltpu.make_async_copy(s, d, small_sem.at[i])
        for i, (s, d) in enumerate(
            ((nsc_h, nsc), (nsh_h, nsh), (be_h, be), (dk_h, dk), (db_h, db), (bp_h, bp),
             (ag_h, ag), (as_h, ash), (bq_h, bq), (bo_h, bo))
        )
    ]
    for s in smalls:
        s.start()
    wide = E // WCHUNKS
    wcopies = [
        pltpu.make_async_copy(
            we_h.at[:, pl.ds(i * wide, wide)], we.at[:, pl.ds(i * wide, wide)], we_sem.at[i]
        )
        for i in range(WCHUNKS)
    ]
    for w in wcopies:
        w.start()

    def signal(i, _):
        pl.semaphore_signal(
            bar, inc=1, device_id=place(lax.rem(me + i, PEERS)), device_id_type=MESH
        )
        return 0

    lax.fori_loop(1, PEERS, signal, 0)
    for dr in (-1, 0, 1):
        for dc in (-1, 1):
            pl.semaphore_signal(
                bar, inc=1,
                device_id=(lax.rem(r + dr + ROWS, ROWS), lax.rem(c + dc + COLS, COLS)),
                device_id_type=MESH,
            )

    bigs = [
        pltpu.make_async_copy(s, d, w_sem.at[i])
        for i, (s, d) in enumerate(((wp_h, wp), (wq_h, wq), (wo_h, wo)))
    ]
    for w in bigs:
        w.start()

    fcopy.wait()
    for s in smalls:
        s.wait()

    def normalise(v):
        return (v.astype(F32) * nsc[...][None, :] + nsh[...][None, :]).astype(BF16)

    def norm_row(h, _):
        xn[pl.ds(pl.multiple_of(h * TC, TC), TC), :] = normalise(feat[h])
        return 0

    lax.fori_loop(0, TR, norm_row, 0)

    def expand_chunk(ci, _):
        cols = pl.ds(pl.multiple_of(ci * 256, 256), 256)
        for mb in range(2):
            acc = jnp.dot(
                xn[mb * 256 : (mb + 1) * 256, :], we[:, cols], preferred_element_type=F32
            )
            g = gelu(acc + be[:, cols]).astype(BF16)
            hid[1 + 4 * mb : 5 + 4 * mb, :, cols] = g.reshape(4, TC, 256)
        return 0

    early = 4
    for i in range(early):
        wcopies[i].wait()
        lax.fori_loop(2 * i, 2 * i + 2, expand_chunk, 0, unroll=2)

    pl.semaphore_wait(bar, PEERS - 1 + 6)

    def halo(src, dst, k, dr, dc):
        return pltpu.make_async_remote_copy(
            src_ref=src, dst_ref=dst, send_sem=halo_ssem.at[k], recv_sem=halo_rsem.at[k],
            device_id=(lax.rem(r + dr + ROWS, ROWS), lax.rem(c + dc + COLS, COLS)),
            device_id_type=MESH,
        )

    halos = [
        halo(feat.at[TR - 1], top, 0, 1, 0),
        halo(feat.at[0], bot, 1, -1, 0),
        halo(feat.at[:, pl.ds(TC - 8, 8)], left, 2, 0, 1),
        halo(feat.at[:, pl.ds(0, 8)], right, 3, 0, -1),
        halo(feat.at[TR - 1, pl.ds(TC - 8, 8)], corner.at[0], 4, 1, 1),
        halo(feat.at[0, pl.ds(TC - 8, 8)], corner.at[1], 5, -1, 1),
        halo(feat.at[TR - 1, pl.ds(0, 8)], corner.at[2], 6, 1, -1),
        halo(feat.at[0, pl.ds(0, 8)], corner.at[3], 7, -1, -1),
    ]
    for h in halos:
        h.start()

    for i in range(early, WCHUNKS):
        wcopies[i].wait()
        lax.fori_loop(2 * i, 2 * i + 2, expand_chunk, 0, unroll=2)

    for h in halos:
        h.wait()

    top_ok = jnp.where(r > 0, 1.0, 0.0).astype(F32)
    bot_ok = jnp.where(r < ROWS - 1, 1.0, 0.0).astype(F32)
    left_ok = jnp.where(c > 0, 1.0, 0.0).astype(F32)
    right_ok = jnp.where(c < COLS - 1, 1.0, 0.0).astype(F32)

    xn[0:TC, :] = normalise(top[...])
    xn[TC : 2 * TC, :] = normalise(bot[...])
    for i in range(TR):
        xblk[i * 8 : i * 8 + 8, :] = normalise(left[i])
        xblk[64 + i * 8 : 64 + i * 8 + 8, :] = normalise(right[i])
    for i in range(4):
        xblk[128 + i * 8 : 136 + i * 8, :] = normalise(corner[i])
    xblk[160:256, :] = jnp.zeros((96, C), BF16)
    t = lax.broadcasted_iota(jnp.int32, (32, 256), 0)
    n = lax.broadcasted_iota(jnp.int32, (32, 256), 1)
    tr = lax.rem(t, 16)
    want_l = jnp.where(tr == 0, 135, jnp.where(tr == 9, 143, (tr - 1) * 8 + 7))
    want_r = jnp.where(tr == 0, 144, jnp.where(tr == 9, 152, 64 + (tr - 1) * 8))
    want = jnp.where(t < 16, want_l, want_r)
    want = jnp.where(tr <= 9, want, -1)
    pick = jnp.where(n == want, 1.0, 0.0).astype(BF16)
    xn[2 * TC : 2 * TC + 32, :] = jnp.dot(
        pick, xblk[...], preferred_element_type=F32
    ).astype(BF16)

    def halo_chunk(ci, _):
        cols = pl.ds(pl.multiple_of(ci * 256, 256), 256)
        acc = jnp.dot(xn[0 : 2 * TC + 32, :], we[:, cols], preferred_element_type=F32)
        g = gelu(acc + be[:, cols])
        hid[0, :, cols] = (g[0:TC] * top_ok).astype(BF16)
        hid[TR + 1, :, cols] = (g[TC : 2 * TC] * bot_ok).astype(BF16)
        gs = g[2 * TC : 2 * TC + 32].astype(BF16).astype(F32)
        ti = lax.broadcasted_iota(jnp.int32, (16, 256), 0)
        edge = jnp.where(ti == 0, top_ok, jnp.where(ti == 9, bot_ok, 1.0))
        gl = gs[0:16] * (edge * left_ok)
        gr = gs[16:32] * (edge * right_ok)
        kl = [dk[a, 0:1, cols] for a in range(3)]
        kr = [dk[a, 2:3, cols] for a in range(3)]
        ledge = gl[0:8] * kl[0] + gl[1:9] * kl[1] + gl[2:10] * kl[2]
        redge = gr[0:8] * kr[0] + gr[1:9] * kr[1] + gr[2:10] * kr[2]
        for i in range(TR):
            hl[i, :, cols] = jnp.broadcast_to(ledge[i : i + 1], (8, 256))
            hr[i, :, cols] = jnp.broadcast_to(redge[i : i + 1], (8, 256))
        return 0

    lax.fori_loop(0, E // 256, halo_chunk, 0, unroll=3)

    bigs[0].wait()
    sub_id = lax.broadcasted_iota(jnp.int32, (8, 128), 0)

    def send_chunk(p):
        return pltpu.make_async_remote_copy(
            src_ref=send.at[p], dst_ref=recv.at[me], send_sem=a_ssem, recv_sem=a_rsem,
            device_id=place(p), device_id_type=MESH,
        )

    def block(k, _):
        b = (k + (me >> 4)) & 3

        def depthwise(ci):
            for half in range(2):
                cols = pl.ds(pl.multiple_of(ci * 256 + half * 128, 128), 128)
                rows = [hid[2 * b + i, :, cols].astype(F32) for i in range(4)]
                bias = db[:, cols]
                taps = [[dk[a, q : q + 1, cols] for q in range(3)] for a in range(3)]
                for o in range(2):
                    s = [
                        rows[o] * taps[0][q] + rows[o + 1] * taps[1][q] + rows[o + 2] * taps[2][q]
                        for q in range(3)
                    ]
                    down = pltpu.roll(s[0], 1, 0)
                    up = pltpu.roll(s[2], TC - 1, 0)
                    first = jnp.where(sub_id == 0, hl[2 * b + o, :, cols], down[0:8])
                    last = jnp.where(sub_id == 7, hr[2 * b + o, :, cols], up[TC - 8 : TC])
                    total = (
                        s[1] + bias
                        + jnp.concatenate([first, down[8:TC]], axis=0)
                        + jnp.concatenate([up[0 : TC - 8], last], axis=0)
                    )
                    dwb[o * TC : (o + 1) * TC, cols] = gelu(total).astype(BF16)

        def project(ci):
            part = pl.ds(pl.multiple_of(ci * 256, 256), 256)
            acc[...] += jnp.dot(dwb[:, part], wp[part, :], preferred_element_type=F32)

        def lane(ci, _):
            project(ci - 1)
            depthwise(ci)
            return 0

        acc[...] = jnp.broadcast_to(bp[...][None, :], (2 * TC, C))
        depthwise(0)
        lax.fori_loop(1, E // 256, lane, 0)
        project(E // 256 - 1)
        proj = acc[...]
        f0 = feat[2 * b].astype(F32)
        f1 = feat[2 * b + 1].astype(F32)
        for o, f in ((0, f0), (1, f1)):
            acb = (f + proj[o * TC : (o + 1) * TC]).astype(BF16)
            feat[2 * b + o] = acb
            wide_ac = acb.astype(F32)
            center = wide_ac - jnp.mean(wide_ac, axis=-1, keepdims=True)
            spread = jnp.mean(center * center, axis=-1, keepdims=True)
            y = (center * lax.rsqrt(spread + 1e-06) * ag[...][None, :] + ash[...][None, :]).astype(BF16)
            send[pl.ds((2 * b + o) * 8, 8)] = y.reshape(8, 8, C)

        def go(j, _):
            p = 16 * b + lax.rem(j + me, 16)

            @pl.when(p != me)
            def _():
                send_chunk(p).start()

            return 0

        lax.fori_loop(0, 16, go, 0, unroll=8)
        return 0

    lax.fori_loop(0, 4, block, 0)
    accopy = pltpu.make_async_copy(feat, ac_out, out_sem)
    accopy.start()
    recv[pl.ds(me, 1)] = send[pl.ds(me, 1)]
    ri = lax.broadcasted_iota(jnp.int32, (256, 256), 0) >> 6
    rj = lax.broadcasted_iota(jnp.int32, (256, 256), 1) >> 6
    ones[...] = jnp.where(ri == rj, 1.0, 0.0).astype(BF16)
    bigs[1].wait()
    bigs[2].wait()
    pltpu.make_async_copy(send.at[pl.ds(0, PEERS - 1)], send.at[pl.ds(0, PEERS - 1)], a_ssem).wait()
    pltpu.make_async_copy(recv.at[pl.ds(0, PEERS - 1)], recv.at[pl.ds(0, PEERS - 1)], a_rsem).wait()

    lane_head = lax.broadcasted_iota(jnp.int32, (64, 128), 1) >> 5
    masks = [jnp.where(lane_head == i, 1.0, 0.0).astype(BF16) for i in range(4)]

    def return_chunk(p, sub):
        return pltpu.make_async_remote_copy(
            src_ref=retbuf.at[sub, p], dst_ref=ret_out.at[me, pl.ds(PER * sub, PER)],
            send_sem=b_ssem, recv_sem=b_rsem, device_id=place(p), device_id_type=MESH,
        )

    subrows = PER * PEERS

    for sub in range(NSUB):
        m = lax.broadcasted_iota(jnp.int32, (subrows, TOKENS), 0)
        nn = lax.broadcasted_iota(jnp.int32, (subrows, TOKENS), 1)
        perm = jnp.where(nn == (m & 63) * 8 + (m >> 6) + PER * sub, 1.0, 0.0).astype(BF16)
        xp[...] = jnp.dot(
            perm, recv[...].reshape(TOKENS, C), preferred_element_type=F32
        ).astype(BF16)

        def qkv_chunk(ci, _):
            cols = pl.ds(pl.multiple_of(ci * 256, 256), 256)
            part = jnp.dot(xp[...], wq[:, cols], preferred_element_type=F32)
            qkv[:, cols] = (part + bq[cols][None, :]).astype(BF16)
            if sub > 0:
                for j in range(7):
                    return_chunk((ci * 7 + j + 1 + me) & (PEERS - 1), sub - 1).start()
            return 0

        lax.fori_loop(0, 9, qkv_chunk, 0, unroll=9)

        def group(g, _):
            rows = pl.ds(pl.multiple_of(g * 64, 64), 64)
            es = []
            for quad in range(QUADS):
                lo = quad * 128
                q = qkv[rows, lo : lo + 128]
                kk = qkv[rows, C + lo : C + lo + 128]
                kbd = jnp.concatenate([kk * m for m in masks], axis=0)
                s = lax.dot_general(
                    q, kbd, (((1,), (1,)), ((), ())), preferred_element_type=F32
                )
                es.append(jnp.exp2(s * EXP_SCALE))
            e = jnp.concatenate(es, axis=0)
            tot = jnp.dot(e.astype(BF16), ones[...], preferred_element_type=F32)
            probs = (e / tot).astype(BF16)
            for quad in range(QUADS):
                lo = quad * 128
                vv = qkv[rows, 2 * C + lo : 2 * C + lo + 128]
                vbd = jnp.concatenate([vv * m for m in masks], axis=0)
                o = jnp.dot(
                    probs[quad * 64 : (quad + 1) * 64], vbd, preferred_element_type=F32
                )
                mixed[rows, lo : lo + 128] = o.astype(BF16)
            return 0

        lax.fori_loop(0, PER, group, 0, unroll=4)
        m = lax.broadcasted_iota(jnp.int32, (subrows, subrows), 0)
        nn = lax.broadcasted_iota(jnp.int32, (subrows, subrows), 1)
        back = jnp.where(
            nn == (m & (PER - 1)) * 64 + (m >> PER_BITS), 1.0, 0.0
        ).astype(BF16)
        mm = jnp.dot(back, mixed[...], preferred_element_type=F32).astype(BF16)
        y = (jnp.dot(mm, wo[...], preferred_element_type=F32) + bo[...][None, :]).astype(BF16)
        retbuf[sub] = y.reshape(PEERS, PER, C)
        pltpu.make_async_copy(
            retbuf.at[sub, me], ret_out.at[me, pl.ds(PER * sub, PER)], self_sem.at[sub]
        ).start()

        def go(j, _):
            return_chunk(lax.rem(j + me, PEERS), sub).start()
            return 0

        if sub == NSUB - 1:
            lax.fori_loop(1, PEERS, go, 0, unroll=21)

    for sub in range(NSUB):
        pltpu.make_async_copy(
            retbuf.at[sub, me], ret_out.at[me, pl.ds(PER * sub, PER)], self_sem.at[sub]
        ).wait()
    accopy.wait()
    pltpu.make_async_copy(ret_out.at[pl.ds(0, PEERS - 1)], ret_out.at[pl.ds(0, PEERS - 1)], b_ssem).wait()
    pltpu.make_async_copy(ret_out.at[pl.ds(0, PEERS - 1)], ret_out.at[pl.ds(0, PEERS - 1)], b_rsem).wait()


def per_device(
    features, norm_scale, norm_shift, expand_weight, expand_bias, depth_kernel, depth_bias,
    project_weight, project_bias, attn_gain, attn_shift, qkv_weight, qkv_bias, out_weight, out_bias,
):
    row = lambda v: v if v.shape[0] % 1024 else v.reshape(1, -1)
    args = (
        features, row(norm_scale), row(norm_shift), expand_weight, row(expand_bias), depth_kernel,
        row(depth_bias), project_weight, row(project_bias), row(attn_gain), row(attn_shift),
        qkv_weight, row(qkv_bias), out_weight, row(out_bias),
    )
    vm = pltpu.VMEM
    dma = pltpu.SemaphoreType.DMA
    scratch = [vm(a.shape, a.dtype) for a in args]
    scratch += [
        vm((TOKENS, C), BF16),
        vm((TC, C), BF16),
        vm((TC, C), BF16),
        vm((TR, 8, C), BF16),
        vm((TR, 8, C), BF16),
        vm((4, 8, C), BF16),
        vm((256, C), BF16),
        vm((TR + 2, TC, E), BF16),
        vm((TR, 8, E), F32),
        vm((TR, 8, E), F32),
        vm((2 * TC, E), BF16),
        vm((PEERS, 8, C), BF16),
        vm((PEERS, 8, C), BF16),
        vm((TOKENS // NSUB, C), BF16),
        vm((TOKENS // NSUB, 3 * C), BF16),
        vm((TOKENS // NSUB, C), BF16),
        vm((NSUB, PEERS, PER, C), BF16),
        vm((2 * TC, C), F32),
        vm((256, 256), BF16),
        dma((10,)), dma, dma((WCHUNKS,)), dma((3,)), dma((8,)), dma((8,)),
        dma, dma, dma, dma, dma, dma((NSUB,)),
    ]
    hbm = pl.BlockSpec(memory_space=pl.ANY)
    after_conv, attended = pl.pallas_call(
        kernel,
        out_shape=(
            jax.ShapeDtypeStruct((TR, TC, C), BF16),
            jax.ShapeDtypeStruct((PEERS, 8, C), BF16),
        ),
        in_specs=[hbm] * len(args),
        out_specs=(hbm, hbm),
        scratch_shapes=scratch,
        name="block",
        compiler_params=pltpu.CompilerParams(
            collective_id=0, has_side_effects=True, vmem_limit_bytes=60 << 20
        ),
    )(*args)
    return (after_conv.astype(F32) + attended.reshape(after_conv.shape).astype(F32)).astype(BF16)


def solution(mesh):
    return jax.shard_map(
        per_device,
        mesh=mesh,
        in_specs=(P("row", "col", None),) + (P(),) * 14,
        out_specs=P("row", "col", None),
        check_vma=False,
    )
```

```python
import math

import jax
import jax.numpy as jnp
from jax import lax
from jax.experimental import pallas as pl
from jax.experimental.pallas import tpu as pltpu
from jax.sharding import PartitionSpec as P

MESH = pl.DeviceIdType.MESH
F32 = jnp.float32
BF16 = jnp.bfloat16

ROWS, COLS = 8, 16
PEERS = 64
TR, TC = 8, 64
TOKENS = TR * TC
C = 768
E = 3072
HEAD_DIM = 32
QUADS = 6
NSUB = 2
PER = 8 // NSUB
PER_BITS = PER.bit_length() - 1
WCHUNKS = 6
GC1 = math.sqrt(2.0 / math.pi)
GC2 = GC1 * 0.044715
EXP_SCALE = math.log2(math.e) / math.sqrt(HEAD_DIM)


def gelu(v):
    half = 0.5 * v
    return half + half * jnp.tanh(v * (GC1 + GC2 * (v * v)))


def kernel(
    f_hbm, nsc_h, nsh_h, we_h, be_h, dk_h, db_h, wp_h, bp_h, ag_h, as_h, wq_h, bq_h, wo_h, bo_h,
    ac_out, ret_out,
    feat, nsc, nsh, we, be, dk, db, wp, bp, ag, ash, wq, bq, wo, bo,
    xn, top, bot, left, right, corner, xblk, hid, hl, hr, dwb, send, recv, xp, qkv, mixed, retbuf, acc, ones,
    small_sem, feat_sem, we_sem, w_sem, halo_ssem, halo_rsem, a_ssem, a_rsem, b_ssem, b_rsem, out_sem, self_sem,
):
    r = lax.axis_index("row")
    c = lax.axis_index("col")
    core = c & 1
    x, y, z = r & 3, ((r >> 2) << 1) + ((c >> 1) & 1), c >> 2
    me = (((x + y + z) & 3) << 4) + (y << 2) + z

    def place(k):
        y, z = (k >> 2) & 3, k & 3
        x = ((k >> 4) - y - z) & 3
        return (((y >> 1) << 2) + x, (z << 2) + ((y & 1) << 1) + core)

    bar = pltpu.get_barrier_semaphore()

    fcopy = pltpu.make_async_copy(f_hbm, feat, feat_sem)
    fcopy.start()
    smalls = [
        pltpu.make_async_copy(s, d, small_sem.at[i])
        for i, (s, d) in enumerate(
            ((nsc_h, nsc), (nsh_h, nsh), (be_h, be), (dk_h, dk), (db_h, db), (bp_h, bp),
             (ag_h, ag), (as_h, ash), (bq_h, bq), (bo_h, bo))
        )
    ]
    for s in smalls:
        s.start()
    wide = E // WCHUNKS
    wcopies = [
        pltpu.make_async_copy(
            we_h.at[:, pl.ds(i * wide, wide)], we.at[:, pl.ds(i * wide, wide)], we_sem.at[i]
        )
        for i in range(WCHUNKS)
    ]
    for w in wcopies:
        w.start()

    def signal(i, _):
        pl.semaphore_signal(
            bar, inc=1, device_id=place(lax.rem(me + i, PEERS)), device_id_type=MESH
        )
        return 0

    lax.fori_loop(1, PEERS, signal, 0)
    for dr in (-1, 0, 1):
        for dc in (-1, 1):
            pl.semaphore_signal(
                bar, inc=1,
                device_id=(lax.rem(r + dr + ROWS, ROWS), lax.rem(c + dc + COLS, COLS)),
                device_id_type=MESH,
            )

    bigs = [
        pltpu.make_async_copy(s, d, w_sem.at[i])
        for i, (s, d) in enumerate(((wp_h, wp), (wq_h, wq), (wo_h, wo)))
    ]
    for w in bigs:
        w.start()

    fcopy.wait()
    for s in smalls:
        s.wait()

    def normalise(v):
        return (v.astype(F32) * nsc[...][None, :] + nsh[...][None, :]).astype(BF16)

    def norm_row(h, _):
        xn[pl.ds(pl.multiple_of(h * TC, TC), TC), :] = normalise(feat[h])
        return 0

    lax.fori_loop(0, TR, norm_row, 0)

    def expand_chunk(ci, _):
        cols = pl.ds(pl.multiple_of(ci * 256, 256), 256)
        for mb in range(2):
            acc = jnp.dot(
                xn[mb * 256 : (mb + 1) * 256, :], we[:, cols], preferred_element_type=F32
            )
            g = gelu((acc + be[:, cols]).astype(BF16))
            hid[1 + 4 * mb : 5 + 4 * mb, :, cols] = g.reshape(4, TC, 256)
        return 0

    early = 1
    for i in range(early):
        wcopies[i].wait()
        lax.fori_loop(2 * i, 2 * i + 2, expand_chunk, 0, unroll=2)

    pl.semaphore_wait(bar, PEERS - 1 + 6)

    def halo(src, dst, k, dr, dc):
        return pltpu.make_async_remote_copy(
            src_ref=src, dst_ref=dst, send_sem=halo_ssem.at[k], recv_sem=halo_rsem.at[k],
            device_id=(lax.rem(r + dr + ROWS, ROWS), lax.rem(c + dc + COLS, COLS)),
            device_id_type=MESH,
        )

    halos = [
        halo(feat.at[TR - 1], top, 0, 1, 0),
        halo(feat.at[0], bot, 1, -1, 0),
        halo(feat.at[:, pl.ds(TC - 4, 4)], left.at[:, pl.ds(4, 4)], 2, 0, 1),
        halo(feat.at[:, pl.ds(0, 4)], right.at[:, pl.ds(0, 4)], 3, 0, -1),
        halo(feat.at[TR - 1, pl.ds(TC - 4, 4)], corner.at[0, pl.ds(4, 4)], 4, 1, 1),
        halo(feat.at[0, pl.ds(TC - 4, 4)], corner.at[1, pl.ds(4, 4)], 5, -1, 1),
        halo(feat.at[TR - 1, pl.ds(0, 4)], corner.at[2, pl.ds(0, 4)], 6, 1, -1),
        halo(feat.at[0, pl.ds(0, 4)], corner.at[3, pl.ds(0, 4)], 7, -1, -1),
    ]
    for h in halos:
        h.start()

    for i in range(early, WCHUNKS):
        wcopies[i].wait()
        lax.fori_loop(2 * i, 2 * i + 2, expand_chunk, 0, unroll=2)

    for h in halos:
        h.wait()

    top_ok = jnp.where(r > 0, 1.0, 0.0).astype(F32)
    bot_ok = jnp.where(r < ROWS - 1, 1.0, 0.0).astype(F32)
    left_ok = jnp.where(c > 0, 1.0, 0.0).astype(F32)
    right_ok = jnp.where(c < COLS - 1, 1.0, 0.0).astype(F32)

    xn[0:TC, :] = normalise(top[...])
    xn[TC : 2 * TC, :] = normalise(bot[...])
    for i in range(TR):
        xblk[i * 8 : i * 8 + 8, :] = normalise(left[i])
        xblk[64 + i * 8 : 64 + i * 8 + 8, :] = normalise(right[i])
    for i in range(4):
        xblk[128 + i * 8 : 136 + i * 8, :] = normalise(corner[i])
    xblk[160:256, :] = jnp.zeros((96, C), BF16)
    t = lax.broadcasted_iota(jnp.int32, (32, 256), 0)
    n = lax.broadcasted_iota(jnp.int32, (32, 256), 1)
    tr = lax.rem(t, 16)
    want_l = jnp.where(tr == 0, 135, jnp.where(tr == 9, 143, (tr - 1) * 8 + 7))
    want_r = jnp.where(tr == 0, 144, jnp.where(tr == 9, 152, 64 + (tr - 1) * 8))
    want = jnp.where(t < 16, want_l, want_r)
    want = jnp.where(tr <= 9, want, -1)
    pick = jnp.where(n == want, 1.0, 0.0).astype(BF16)
    xn[2 * TC : 2 * TC + 32, :] = jnp.dot(
        pick, xblk[...], preferred_element_type=F32
    ).astype(BF16)

    def halo_chunk(ci, _):
        cols = pl.ds(pl.multiple_of(ci * 256, 256), 256)
        acc = jnp.dot(xn[0 : 2 * TC + 32, :], we[:, cols], preferred_element_type=F32)
        g = gelu(acc + be[:, cols])
        hid[0, :, cols] = (g[0:TC] * top_ok).astype(BF16)
        hid[TR + 1, :, cols] = (g[TC : 2 * TC] * bot_ok).astype(BF16)
        gs = g[2 * TC : 2 * TC + 32].astype(BF16).astype(F32)
        ti = lax.broadcasted_iota(jnp.int32, (16, 256), 0)
        edge = jnp.where(ti == 0, top_ok, jnp.where(ti == 9, bot_ok, 1.0))
        gl = gs[0:16] * (edge * left_ok)
        gr = gs[16:32] * (edge * right_ok)
        kl = [dk[a, 0:1, cols] for a in range(3)]
        kr = [dk[a, 2:3, cols] for a in range(3)]
        ledge = gl[0:8] * kl[0] + gl[1:9] * kl[1] + gl[2:10] * kl[2]
        redge = gr[0:8] * kr[0] + gr[1:9] * kr[1] + gr[2:10] * kr[2]
        for i in range(TR):
            hl[i, :, cols] = jnp.broadcast_to(ledge[i : i + 1], (8, 256))
            hr[i, :, cols] = jnp.broadcast_to(redge[i : i + 1], (8, 256))
        return 0

    lax.fori_loop(0, E // 256, halo_chunk, 0, unroll=3)

    bigs[0].wait()
    sub_id = lax.broadcasted_iota(jnp.int32, (8, 128), 0)

    def send_chunk(p):
        return pltpu.make_async_remote_copy(
            src_ref=send.at[p], dst_ref=recv.at[me], send_sem=a_ssem, recv_sem=a_rsem,
            device_id=place(p), device_id_type=MESH,
        )

    def block(k, _):
        b = (k + (me >> 4)) & 3

        def depthwise(ci):
            for half in range(2):
                cols = pl.ds(pl.multiple_of(ci * 256 + half * 128, 128), 128)
                rows = [hid[2 * b + i, :, cols].astype(F32) for i in range(4)]
                bias = db[:, cols]
                taps = [[dk[a, q : q + 1, cols] for q in range(3)] for a in range(3)]
                for o in range(2):
                    s = [
                        rows[o] * taps[0][q] + rows[o + 1] * taps[1][q] + rows[o + 2] * taps[2][q]
                        for q in range(3)
                    ]
                    down = pltpu.roll(s[0], 1, 0)
                    up = pltpu.roll(s[2], TC - 1, 0)
                    first = jnp.where(sub_id == 0, hl[2 * b + o, :, cols], down[0:8])
                    last = jnp.where(sub_id == 7, hr[2 * b + o, :, cols], up[TC - 8 : TC])
                    total = (
                        s[1] + bias
                        + jnp.concatenate([first, down[8:TC]], axis=0)
                        + jnp.concatenate([up[0 : TC - 8], last], axis=0)
                    )
                    dwb[o * TC : (o + 1) * TC, cols] = gelu(total.astype(BF16))

        def project(ci):
            part = pl.ds(pl.multiple_of(ci * 256, 256), 256)
            acc[...] += jnp.dot(dwb[:, part], wp[part, :], preferred_element_type=F32)

        def lane(ci, _):
            project(ci - 1)
            depthwise(ci)
            return 0

        acc[...] = jnp.broadcast_to(bp[...][None, :], (2 * TC, C))
        depthwise(0)
        lax.fori_loop(1, E // 256, lane, 0)
        project(E // 256 - 1)
        proj = acc[...]
        f0 = feat[2 * b].astype(F32)
        f1 = feat[2 * b + 1].astype(F32)
        for o, f in ((0, f0), (1, f1)):
            acb = (f + proj[o * TC : (o + 1) * TC]).astype(BF16)
            feat[2 * b + o] = acb
            wide_ac = acb.astype(F32)
            center = wide_ac - jnp.mean(wide_ac, axis=-1, keepdims=True)
            spread = jnp.mean(center * center, axis=-1, keepdims=True)
            y = (center * lax.rsqrt(spread + 1e-06) * ag[...][None, :] + ash[...][None, :]).astype(BF16)
            send[pl.ds((2 * b + o) * 8, 8)] = y.reshape(8, 8, C)

        def go(j, _):
            p = 16 * b + lax.rem(j + me, 16)

            @pl.when(p != me)
            def _():
                send_chunk(p).start()

            return 0

        lax.fori_loop(0, 16, go, 0, unroll=8)
        return 0

    lax.fori_loop(0, 4, block, 0)
    accopy = pltpu.make_async_copy(feat, ac_out, out_sem)
    accopy.start()
    recv[pl.ds(me, 1)] = send[pl.ds(me, 1)]
    ri = lax.broadcasted_iota(jnp.int32, (256, 256), 0) >> 6
    rj = lax.broadcasted_iota(jnp.int32, (256, 256), 1) >> 6
    ones[...] = jnp.where(ri == rj, 1.0, 0.0).astype(BF16)
    bigs[1].wait()
    bigs[2].wait()
    pltpu.make_async_copy(send.at[pl.ds(0, PEERS - 1)], send.at[pl.ds(0, PEERS - 1)], a_ssem).wait()
    pltpu.make_async_copy(recv.at[pl.ds(0, PEERS - 1)], recv.at[pl.ds(0, PEERS - 1)], a_rsem).wait()

    lane_head = lax.broadcasted_iota(jnp.int32, (64, 128), 1) >> 5
    masks = [jnp.where(lane_head == i, 1.0, 0.0).astype(BF16) for i in range(4)]

    def return_chunk(p, sub):
        return pltpu.make_async_remote_copy(
            src_ref=retbuf.at[sub, p], dst_ref=ret_out.at[me, pl.ds(PER * sub, PER)],
            send_sem=b_ssem, recv_sem=b_rsem, device_id=place(p), device_id_type=MESH,
        )

    subrows = PER * PEERS

    for sub in range(NSUB):
        m = lax.broadcasted_iota(jnp.int32, (subrows, TOKENS), 0)
        nn = lax.broadcasted_iota(jnp.int32, (subrows, TOKENS), 1)
        perm = jnp.where(nn == (m & 63) * 8 + (m >> 6) + PER * sub, 1.0, 0.0).astype(BF16)
        xp[...] = jnp.dot(
            perm, recv[...].reshape(TOKENS, C), preferred_element_type=F32
        ).astype(BF16)

        def qkv_chunk(ci, _):
            cols = pl.ds(pl.multiple_of(ci * 256, 256), 256)
            part = jnp.dot(xp[...], wq[:, cols], preferred_element_type=F32)
            qkv[:, cols] = (part + bq[cols][None, :]).astype(BF16)
            if sub > 0:
                for j in range(7):
                    return_chunk((ci * 7 + j + 1 + me) & (PEERS - 1), sub - 1).start()
            return 0

        lax.fori_loop(0, 9, qkv_chunk, 0, unroll=9)

        def group(g, _):
            rows = pl.ds(pl.multiple_of(g * 64, 64), 64)
            es = []
            for quad in range(QUADS):
                lo = quad * 128
                q = qkv[rows, lo : lo + 128]
                kk = qkv[rows, C + lo : C + lo + 128]
                kbd = jnp.concatenate([kk * m for m in masks], axis=0)
                s = lax.dot_general(
                    q, kbd, (((1,), (1,)), ((), ())), preferred_element_type=F32
                )
                es.append(jnp.exp2(s * EXP_SCALE))
            e = jnp.concatenate(es, axis=0)
            tot = jnp.dot(e.astype(BF16), ones[...], preferred_element_type=F32)
            probs = (e / tot).astype(BF16)
            for quad in range(QUADS):
                lo = quad * 128
                vv = qkv[rows, 2 * C + lo : 2 * C + lo + 128]
                vbd = jnp.concatenate([vv * m for m in masks], axis=0)
                o = jnp.dot(
                    probs[quad * 64 : (quad + 1) * 64], vbd, preferred_element_type=F32
                )
                mixed[rows, lo : lo + 128] = o.astype(BF16)
            return 0

        lax.fori_loop(0, PER, group, 0, unroll=4)
        m = lax.broadcasted_iota(jnp.int32, (subrows, subrows), 0)
        nn = lax.broadcasted_iota(jnp.int32, (subrows, subrows), 1)
        back = jnp.where(
            nn == (m & (PER - 1)) * 64 + (m >> PER_BITS), 1.0, 0.0
        ).astype(BF16)
        mm = jnp.dot(back, mixed[...], preferred_element_type=F32).astype(BF16)
        y = (jnp.dot(mm, wo[...], preferred_element_type=F32) + bo[...][None, :]).astype(BF16)
        retbuf[sub] = y.reshape(PEERS, PER, C)
        pltpu.make_async_copy(
            retbuf.at[sub, me], ret_out.at[me, pl.ds(PER * sub, PER)], self_sem.at[sub]
        ).start()

        def go(j, _):
            return_chunk(lax.rem(j + me, PEERS), sub).start()
            return 0

        if sub == NSUB - 1:
            lax.fori_loop(1, PEERS, go, 0, unroll=21)

    for sub in range(NSUB):
        pltpu.make_async_copy(
            retbuf.at[sub, me], ret_out.at[me, pl.ds(PER * sub, PER)], self_sem.at[sub]
        ).wait()
    accopy.wait()
    pltpu.make_async_copy(ret_out.at[pl.ds(0, PEERS - 1)], ret_out.at[pl.ds(0, PEERS - 1)], b_ssem).wait()
    pltpu.make_async_copy(ret_out.at[pl.ds(0, PEERS - 1)], ret_out.at[pl.ds(0, PEERS - 1)], b_rsem).wait()


def per_device(
    features, norm_scale, norm_shift, expand_weight, expand_bias, depth_kernel, depth_bias,
    project_weight, project_bias, attn_gain, attn_shift, qkv_weight, qkv_bias, out_weight, out_bias,
):
    row = lambda v: v if v.shape[0] % 1024 else v.reshape(1, -1)
    args = (
        features, row(norm_scale), row(norm_shift), expand_weight, row(expand_bias), depth_kernel,
        row(depth_bias), project_weight, row(project_bias), row(attn_gain), row(attn_shift),
        qkv_weight, row(qkv_bias), out_weight, row(out_bias),
    )
    vm = pltpu.VMEM
    dma = pltpu.SemaphoreType.DMA
    scratch = [vm(a.shape, a.dtype) for a in args]
    scratch += [
        vm((TOKENS, C), BF16),
        vm((TC, C), BF16),
        vm((TC, C), BF16),
        vm((TR, 8, C), BF16),
        vm((TR, 8, C), BF16),
        vm((4, 8, C), BF16),
        vm((256, C), BF16),
        vm((TR + 2, TC, E), BF16),
        vm((TR, 8, E), F32),
        vm((TR, 8, E), F32),
        vm((2 * TC, E), BF16),
        vm((PEERS, 8, C), BF16),
        vm((PEERS, 8, C), BF16),
        vm((TOKENS // NSUB, C), BF16),
        vm((TOKENS // NSUB, 3 * C), BF16),
        vm((TOKENS // NSUB, C), BF16),
        vm((NSUB, PEERS, PER, C), BF16),
        vm((2 * TC, C), F32),
        vm((256, 256), BF16),
        dma((10,)), dma, dma((WCHUNKS,)), dma((3,)), dma((8,)), dma((8,)),
        dma, dma, dma, dma, dma, dma((NSUB,)),
    ]
    hbm = pl.BlockSpec(memory_space=pl.ANY)
    after_conv, attended = pl.pallas_call(
        kernel,
        out_shape=(
            jax.ShapeDtypeStruct((TR, TC, C), BF16),
            jax.ShapeDtypeStruct((PEERS, 8, C), BF16),
        ),
        in_specs=[hbm] * len(args),
        out_specs=(hbm, hbm),
        scratch_shapes=scratch,
        name="block",
        compiler_params=pltpu.CompilerParams(
            collective_id=0, has_side_effects=True, vmem_limit_bytes=60 << 20
        ),
    )(*args)
    return (after_conv.astype(F32) + attended.reshape(after_conv.shape).astype(F32)).astype(BF16)


def solution(mesh):
    return jax.shard_map(
        per_device,
        mesh=mesh,
        in_specs=(P("row", "col", None),) + (P(),) * 14,
        out_specs=P("row", "col", None),
        check_vma=False,
    )
```

```python
import math

import jax
import jax.numpy as jnp
from jax import lax
from jax.experimental import pallas as pl
from jax.experimental.pallas import tpu as pltpu
from jax.sharding import PartitionSpec as P

MESH = pl.DeviceIdType.MESH
F32 = jnp.float32
BF16 = jnp.bfloat16

ROWS, COLS = 8, 16
PEERS = 64
TR, TC = 8, 64
TOKENS = TR * TC
C = 768
E = 3072
HEAD_DIM = 32
QUADS = 6
NSUB = 2
PER = 8 // NSUB
PER_BITS = PER.bit_length() - 1
WCHUNKS = 6
GC1 = math.sqrt(2.0 / math.pi)
GC2 = GC1 * 0.044715
EXP_SCALE = math.log2(math.e) / math.sqrt(HEAD_DIM)


def gelu(v):
    half = 0.5 * v
    return half + half * jnp.tanh(v * (GC1 + GC2 * (v * v)))


def kernel(
    f_hbm, nsc_h, nsh_h, we_h, be_h, dk_h, db_h, wp_h, bp_h, ag_h, as_h, wq_h, bq_h, wo_h, bo_h,
    ac_out, ret_out,
    feat, nsc, nsh, we, be, dk, db, wp, bp, ag, ash, wq, bq, wo, bo,
    xn, top, bot, left, right, corner, xblk, hid, hl, hr, dwb, send, recv, xp, qkv, mixed, retbuf, acc, ones,
    small_sem, feat_sem, we_sem, w_sem, halo_ssem, halo_rsem, a_ssem, a_rsem, b_ssem, b_rsem, out_sem, self_sem,
):
    r = lax.axis_index("row")
    c = lax.axis_index("col")
    core = c & 1
    x, y, z = r & 3, ((r >> 2) << 1) + ((c >> 1) & 1), c >> 2
    me = (((x + y + z) & 3) << 4) + (y << 2) + z

    def place(k):
        y, z = (k >> 2) & 3, k & 3
        x = ((k >> 4) - y - z) & 3
        return (((y >> 1) << 2) + x, (z << 2) + ((y & 1) << 1) + core)

    bar = pltpu.get_barrier_semaphore()

    fcopy = pltpu.make_async_copy(f_hbm, feat, feat_sem)
    fcopy.start()
    smalls = [
        pltpu.make_async_copy(s, d, small_sem.at[i])
        for i, (s, d) in enumerate(
            ((nsc_h, nsc), (nsh_h, nsh), (be_h, be), (dk_h, dk), (db_h, db), (bp_h, bp),
             (ag_h, ag), (as_h, ash), (bq_h, bq), (bo_h, bo))
        )
    ]
    for s in smalls:
        s.start()
    wide = E // WCHUNKS
    wcopies = [
        pltpu.make_async_copy(
            we_h.at[:, pl.ds(i * wide, wide)], we.at[:, pl.ds(i * wide, wide)], we_sem.at[i]
        )
        for i in range(WCHUNKS)
    ]
    for w in wcopies:
        w.start()

    def signal(i, _):
        pl.semaphore_signal(
            bar, inc=1, device_id=place(lax.rem(me + i, PEERS)), device_id_type=MESH
        )
        return 0

    lax.fori_loop(1, PEERS, signal, 0, unroll=9)
    for dr in (-1, 0, 1):
        for dc in (-1, 1):
            pl.semaphore_signal(
                bar, inc=1,
                device_id=(lax.rem(r + dr + ROWS, ROWS), lax.rem(c + dc + COLS, COLS)),
                device_id_type=MESH,
            )

    fcopy.wait()
    for s in smalls:
        s.wait()

    def normalise(v):
        return (v.astype(F32) * nsc[...][None, :] + nsh[...][None, :]).astype(BF16)

    def norm_row(h, _):
        xn[pl.ds(pl.multiple_of(h * TC, TC), TC), :] = normalise(feat[h])
        return 0

    lax.fori_loop(0, TR, norm_row, 0)

    def expand_chunk(ci, _):
        cols = pl.ds(pl.multiple_of(ci * 256, 256), 256)
        for mb in range(2):
            acc = jnp.dot(
                xn[mb * 256 : (mb + 1) * 256, :], we[:, cols], preferred_element_type=F32
            )
            g = gelu(acc + be[:, cols]).astype(BF16)
            hid[1 + 4 * mb : 5 + 4 * mb, :, cols] = g.reshape(4, TC, 256)
        return 0

    early = 1
    for i in range(early):
        wcopies[i].wait()
        lax.fori_loop(2 * i, 2 * i + 2, expand_chunk, 0, unroll=2)

    bigs = [
        pltpu.make_async_copy(s, d, w_sem.at[i])
        for i, (s, d) in enumerate(((wp_h, wp), (wq_h, wq), (wo_h, wo)))
    ]
    for w in bigs:
        w.start()

    pl.semaphore_wait(bar, PEERS - 1 + 6)

    def halo(src, dst, k, dr, dc):
        return pltpu.make_async_remote_copy(
            src_ref=src, dst_ref=dst, send_sem=halo_ssem.at[k], recv_sem=halo_rsem.at[k],
            device_id=(lax.rem(r + dr + ROWS, ROWS), lax.rem(c + dc + COLS, COLS)),
            device_id_type=MESH,
        )

    halos = [
        halo(feat.at[TR - 1], top, 0, 1, 0),
        halo(feat.at[0], bot, 1, -1, 0),
        halo(feat.at[:, pl.ds(TC - 4, 4)], left.at[:, pl.ds(4, 4)], 2, 0, 1),
        halo(feat.at[:, pl.ds(0, 4)], right.at[:, pl.ds(0, 4)], 3, 0, -1),
        halo(feat.at[TR - 1, pl.ds(TC - 4, 4)], corner.at[0, pl.ds(4, 4)], 4, 1, 1),
        halo(feat.at[0, pl.ds(TC - 4, 4)], corner.at[1, pl.ds(4, 4)], 5, -1, 1),
        halo(feat.at[TR - 1, pl.ds(0, 4)], corner.at[2, pl.ds(0, 4)], 6, 1, -1),
        halo(feat.at[0, pl.ds(0, 4)], corner.at[3, pl.ds(0, 4)], 7, -1, -1),
    ]
    for h in halos:
        h.start()

    for i in range(early, WCHUNKS):
        wcopies[i].wait()
        lax.fori_loop(2 * i, 2 * i + 2, expand_chunk, 0, unroll=2)

    for h in halos:
        h.wait()

    top_ok = jnp.where(r > 0, 1.0, 0.0).astype(F32)
    bot_ok = jnp.where(r < ROWS - 1, 1.0, 0.0).astype(F32)
    left_ok = jnp.where(c > 0, 1.0, 0.0).astype(F32)
    right_ok = jnp.where(c < COLS - 1, 1.0, 0.0).astype(F32)

    xn[0:TC, :] = normalise(top[...])
    xn[TC : 2 * TC, :] = normalise(bot[...])
    for i in range(TR):
        xblk[i * 8 : i * 8 + 8, :] = normalise(left[i])
        xblk[64 + i * 8 : 64 + i * 8 + 8, :] = normalise(right[i])
    for i in range(4):
        xblk[128 + i * 8 : 136 + i * 8, :] = normalise(corner[i])
    xblk[160:256, :] = jnp.zeros((96, C), BF16)
    t = lax.broadcasted_iota(jnp.int32, (32, 256), 0)
    n = lax.broadcasted_iota(jnp.int32, (32, 256), 1)
    tr = lax.rem(t, 16)
    want_l = jnp.where(tr == 0, 135, jnp.where(tr == 9, 143, (tr - 1) * 8 + 7))
    want_r = jnp.where(tr == 0, 144, jnp.where(tr == 9, 152, 64 + (tr - 1) * 8))
    want = jnp.where(t < 16, want_l, want_r)
    want = jnp.where(tr <= 9, want, -1)
    pick = jnp.where(n == want, 1.0, 0.0).astype(BF16)
    xn[2 * TC : 2 * TC + 32, :] = jnp.dot(
        pick, xblk[...], preferred_element_type=F32
    ).astype(BF16)

    def halo_chunk(ci, _):
        cols = pl.ds(pl.multiple_of(ci * 256, 256), 256)
        acc = jnp.dot(xn[0 : 2 * TC + 32, :], we[:, cols], preferred_element_type=F32)
        g = gelu(acc + be[:, cols])
        hid[0, :, cols] = (g[0:TC] * top_ok).astype(BF16)
        hid[TR + 1, :, cols] = (g[TC : 2 * TC] * bot_ok).astype(BF16)
        gs = g[2 * TC : 2 * TC + 32].astype(BF16).astype(F32)
        ti = lax.broadcasted_iota(jnp.int32, (16, 256), 0)
        edge = jnp.where(ti == 0, top_ok, jnp.where(ti == 9, bot_ok, 1.0))
        gl = gs[0:16] * (edge * left_ok)
        gr = gs[16:32] * (edge * right_ok)
        kl = [dk[a, 0:1, cols] for a in range(3)]
        kr = [dk[a, 2:3, cols] for a in range(3)]
        ledge = gl[0:8] * kl[0] + gl[1:9] * kl[1] + gl[2:10] * kl[2]
        redge = gr[0:8] * kr[0] + gr[1:9] * kr[1] + gr[2:10] * kr[2]
        for i in range(TR):
            hl[i, :, cols] = jnp.broadcast_to(ledge[i : i + 1], (8, 256))
            hr[i, :, cols] = jnp.broadcast_to(redge[i : i + 1], (8, 256))
        return 0

    lax.fori_loop(0, E // 256, halo_chunk, 0, unroll=3)

    bigs[0].wait()
    sub_id = lax.broadcasted_iota(jnp.int32, (8, 128), 0)

    def send_chunk(p):
        return pltpu.make_async_remote_copy(
            src_ref=send.at[p], dst_ref=recv.at[me], send_sem=a_ssem, recv_sem=a_rsem,
            device_id=place(p), device_id_type=MESH,
        )

    def block(k, _):
        b = (k + (me >> 4)) & 3

        def depthwise(ci):
            for half in range(2):
                cols = pl.ds(pl.multiple_of(ci * 256 + half * 128, 128), 128)
                rows = [hid[2 * b + i, :, cols].astype(F32) for i in range(4)]
                bias = db[:, cols]
                taps = [[dk[a, q : q + 1, cols] for q in range(3)] for a in range(3)]
                for o in range(2):
                    s = [
                        rows[o] * taps[0][q] + rows[o + 1] * taps[1][q] + rows[o + 2] * taps[2][q]
                        for q in range(3)
                    ]
                    down = pltpu.roll(s[0], 1, 0)
                    up = pltpu.roll(s[2], TC - 1, 0)
                    first = jnp.where(sub_id == 0, hl[2 * b + o, :, cols], down[0:8])
                    last = jnp.where(sub_id == 7, hr[2 * b + o, :, cols], up[TC - 8 : TC])
                    total = (
                        s[1] + bias
                        + jnp.concatenate([first, down[8:TC]], axis=0)
                        + jnp.concatenate([up[0 : TC - 8], last], axis=0)
                    )
                    dwb[o * TC : (o + 1) * TC, cols] = gelu(total.astype(BF16))

        def project(ci):
            part = pl.ds(pl.multiple_of(ci * 256, 256), 256)
            acc[...] += jnp.dot(dwb[:, part], wp[part, :], preferred_element_type=F32)

        def lane(ci, _):
            project(ci - 1)
            depthwise(ci)
            return 0

        acc[...] = jnp.broadcast_to(bp[...][None, :], (2 * TC, C))
        depthwise(0)
        lax.fori_loop(1, E // 256, lane, 0)
        project(E // 256 - 1)
        proj = acc[...]
        f0 = feat[2 * b].astype(F32)
        f1 = feat[2 * b + 1].astype(F32)
        for o, f in ((0, f0), (1, f1)):
            acb = (f + proj[o * TC : (o + 1) * TC]).astype(BF16)
            feat[2 * b + o] = acb
            wide_ac = acb.astype(F32)
            center = wide_ac - jnp.mean(wide_ac, axis=-1, keepdims=True)
            spread = jnp.mean(center * center, axis=-1, keepdims=True)
            y = (center * lax.rsqrt(spread + 1e-06) * ag[...][None, :] + ash[...][None, :]).astype(BF16)
            send[pl.ds((2 * b + o) * 8, 8)] = y.reshape(8, 8, C)

        def go(j, _):
            p = 16 * b + lax.rem(j + me, 16)

            @pl.when(p != me)
            def _():
                send_chunk(p).start()

            return 0

        lax.fori_loop(0, 16, go, 0, unroll=8)
        return 0

    lax.fori_loop(0, 4, block, 0)
    accopy = pltpu.make_async_copy(feat, ac_out, out_sem)
    accopy.start()
    recv[pl.ds(me, 1)] = send[pl.ds(me, 1)]
    ri = lax.broadcasted_iota(jnp.int32, (256, 256), 0) >> 6
    rj = lax.broadcasted_iota(jnp.int32, (256, 256), 1) >> 6
    ones[...] = jnp.where(ri == rj, 1.0, 0.0).astype(BF16)
    bigs[1].wait()
    bigs[2].wait()
    pltpu.make_async_copy(send.at[pl.ds(0, PEERS - 1)], send.at[pl.ds(0, PEERS - 1)], a_ssem).wait()
    pltpu.make_async_copy(recv.at[pl.ds(0, PEERS - 1)], recv.at[pl.ds(0, PEERS - 1)], a_rsem).wait()

    lane_head = lax.broadcasted_iota(jnp.int32, (64, 128), 1) >> 5
    masks = [jnp.where(lane_head == i, 1.0, 0.0).astype(BF16) for i in range(4)]

    def return_chunk(p, sub):
        return pltpu.make_async_remote_copy(
            src_ref=retbuf.at[sub, p], dst_ref=ret_out.at[me, pl.ds(PER * sub, PER)],
            send_sem=b_ssem, recv_sem=b_rsem, device_id=place(p), device_id_type=MESH,
        )

    subrows = PER * PEERS

    for sub in range(NSUB):
        m = lax.broadcasted_iota(jnp.int32, (subrows, TOKENS), 0)
        nn = lax.broadcasted_iota(jnp.int32, (subrows, TOKENS), 1)
        perm = jnp.where(nn == (m & 63) * 8 + (m >> 6) + PER * sub, 1.0, 0.0).astype(BF16)
        xp[...] = jnp.dot(
            perm, recv[...].reshape(TOKENS, C), preferred_element_type=F32
        ).astype(BF16)

        def qkv_chunk(ci, _):
            cols = pl.ds(pl.multiple_of(ci * 256, 256), 256)
            part = jnp.dot(xp[...], wq[:, cols], preferred_element_type=F32)
            qkv[:, cols] = (part + bq[cols][None, :]).astype(BF16)
            if sub > 0:
                for j in range(7):
                    return_chunk((ci * 7 + j + 1 + me) & (PEERS - 1), sub - 1).start()
            return 0

        lax.fori_loop(0, 9, qkv_chunk, 0, unroll=9)

        def group(g, _):
            rows = pl.ds(pl.multiple_of(g * 64, 64), 64)
            es = []
            for quad in range(QUADS):
                lo = quad * 128
                q = qkv[rows, lo : lo + 128]
                kk = qkv[rows, C + lo : C + lo + 128]
                kbd = jnp.concatenate([kk * m for m in masks], axis=0)
                s = lax.dot_general(
                    q, kbd, (((1,), (1,)), ((), ())), preferred_element_type=F32
                )
                es.append(jnp.exp2(s * EXP_SCALE))
            e = jnp.concatenate(es, axis=0)
            tot = jnp.dot(e.astype(BF16), ones[...], preferred_element_type=F32)
            probs = (e / tot).astype(BF16)
            for quad in range(QUADS):
                lo = quad * 128
                vv = qkv[rows, 2 * C + lo : 2 * C + lo + 128]
                vbd = jnp.concatenate([vv * m for m in masks], axis=0)
                o = jnp.dot(
                    probs[quad * 64 : (quad + 1) * 64], vbd, preferred_element_type=F32
                )
                mixed[rows, lo : lo + 128] = o.astype(BF16)
            return 0

        lax.fori_loop(0, PER, group, 0, unroll=4)
        parts = 2 if sub == NSUB - 1 else 1
        span, peers = subrows // parts, PEERS // parts
        m = lax.broadcasted_iota(jnp.int32, (span, subrows), 0)
        nn = lax.broadcasted_iota(jnp.int32, (span, subrows), 1)
        for part in range(parts):
            which = (part + me) & (parts - 1)
            token = m + which * span
            back = jnp.where(
                nn == (token & (PER - 1)) * 64 + (token >> PER_BITS), 1.0, 0.0
            ).astype(BF16)
            mm = jnp.dot(back, mixed[...], preferred_element_type=F32).astype(BF16)
            y = (jnp.dot(mm, wo[...], preferred_element_type=F32) + bo[...][None, :]).astype(BF16)
            retbuf[sub, pl.ds(which * peers, peers)] = y.reshape(peers, PER, C)

            def go(j, _):
                p = which * peers + ((j + me) & (peers - 1))

                @pl.when(p != me)
                def _():
                    return_chunk(p, sub).start()

                return 0

            if sub == NSUB - 1:
                lax.fori_loop(0, peers, go, 0, unroll=8)
        pltpu.make_async_copy(
            retbuf.at[sub, me], ret_out.at[me, pl.ds(PER * sub, PER)], self_sem.at[sub]
        ).start()

    for sub in range(NSUB):
        pltpu.make_async_copy(
            retbuf.at[sub, me], ret_out.at[me, pl.ds(PER * sub, PER)], self_sem.at[sub]
        ).wait()
    accopy.wait()
    pltpu.make_async_copy(ret_out.at[pl.ds(0, PEERS - 1)], ret_out.at[pl.ds(0, PEERS - 1)], b_ssem).wait()
    pltpu.make_async_copy(ret_out.at[pl.ds(0, PEERS - 1)], ret_out.at[pl.ds(0, PEERS - 1)], b_rsem).wait()


def per_device(
    features, norm_scale, norm_shift, expand_weight, expand_bias, depth_kernel, depth_bias,
    project_weight, project_bias, attn_gain, attn_shift, qkv_weight, qkv_bias, out_weight, out_bias,
):
    row = lambda v: v if v.shape[0] % 1024 else v.reshape(1, -1)
    args = (
        features, row(norm_scale), row(norm_shift), expand_weight, row(expand_bias), depth_kernel,
        row(depth_bias), project_weight, row(project_bias), row(attn_gain), row(attn_shift),
        qkv_weight, row(qkv_bias), out_weight, row(out_bias),
    )
    vm = pltpu.VMEM
    dma = pltpu.SemaphoreType.DMA
    scratch = [vm(a.shape, a.dtype) for a in args]
    scratch += [
        vm((TOKENS, C), BF16),
        vm((TC, C), BF16),
        vm((TC, C), BF16),
        vm((TR, 8, C), BF16),
        vm((TR, 8, C), BF16),
        vm((4, 8, C), BF16),
        vm((256, C), BF16),
        vm((TR + 2, TC, E), BF16),
        vm((TR, 8, E), F32),
        vm((TR, 8, E), F32),
        vm((2 * TC, E), BF16),
        vm((PEERS, 8, C), BF16),
        vm((PEERS, 8, C), BF16),
        vm((TOKENS // NSUB, C), BF16),
        vm((TOKENS // NSUB, 3 * C), BF16),
        vm((TOKENS // NSUB, C), BF16),
        vm((NSUB, PEERS, PER, C), BF16),
        vm((2 * TC, C), F32),
        vm((256, 256), BF16),
        dma((10,)), dma, dma((WCHUNKS,)), dma((3,)), dma((8,)), dma((8,)),
        dma, dma, dma, dma, dma, dma((NSUB,)),
    ]
    hbm = pl.BlockSpec(memory_space=pl.ANY)
    after_conv, attended = pl.pallas_call(
        kernel,
        out_shape=(
            jax.ShapeDtypeStruct((TR, TC, C), BF16),
            jax.ShapeDtypeStruct((PEERS, 8, C), BF16),
        ),
        in_specs=[hbm] * len(args),
        out_specs=(hbm, hbm),
        scratch_shapes=scratch,
        name="block",
        compiler_params=pltpu.CompilerParams(
            collective_id=0, has_side_effects=True, vmem_limit_bytes=60 << 20
        ),
    )(*args)
    return (after_conv.astype(F32) + attended.reshape(after_conv.shape).astype(F32)).astype(BF16)


def solution(mesh):
    return jax.shard_map(
        per_device,
        mesh=mesh,
        in_specs=(P("row", "col", None),) + (P(),) * 14,
        out_specs=P("row", "col", None),
        check_vma=False,
    )
```

```python
import math

import jax
import jax.numpy as jnp
from jax import lax
from jax.experimental import pallas as pl
from jax.experimental.pallas import tpu as pltpu
from jax.sharding import PartitionSpec as P

MESH = pl.DeviceIdType.MESH
F32 = jnp.float32
BF16 = jnp.bfloat16

ROWS, COLS = 8, 16
PEERS = 64
TR, TC = 8, 64
TOKENS = TR * TC
C = 768
E = 3072
HEAD_DIM = 32
QUADS = 6
NSUB = 2
PER = 8 // NSUB
PER_BITS = PER.bit_length() - 1
WCHUNKS = 6
GC1 = math.sqrt(2.0 / math.pi)
GC2 = GC1 * 0.044715
EXP_SCALE = math.log2(math.e) / math.sqrt(HEAD_DIM)


def gelu(v):
    half = 0.5 * v
    return half + half * jnp.tanh(v * (GC1 + GC2 * (v * v)))


def kernel(
    f_hbm, nsc_h, nsh_h, we_h, be_h, dk_h, db_h, wp_h, bp_h, ag_h, as_h, wq_h, bq_h, wo_h, bo_h,
    ac_out, ret_out,
    feat, nsc, nsh, we, be, dk, db, wp, bp, ag, ash, wq, bq, wo, bo,
    xn, top, bot, left, right, corner, xblk, hid, hl, hr, dwb, send, recv, xp, qkv, mixed, retbuf, acc, ones,
    small_sem, feat_sem, we_sem, w_sem, halo_ssem, halo_rsem, a_ssem, a_rsem, b_ssem, b_rsem, out_sem, self_sem,
):
    r = lax.axis_index("row")
    c = lax.axis_index("col")
    core = c & 1
    x, y, z = r & 3, ((r >> 2) << 1) + ((c >> 1) & 1), c >> 2
    me = (((x + y + z) & 3) << 4) + (y << 2) + z

    def place(k):
        y, z = (k >> 2) & 3, k & 3
        x = ((k >> 4) - y - z) & 3
        return (((y >> 1) << 2) + x, (z << 2) + ((y & 1) << 1) + core)

    bar = pltpu.get_barrier_semaphore()

    fcopy = pltpu.make_async_copy(f_hbm, feat, feat_sem)
    fcopy.start()
    smalls = [
        pltpu.make_async_copy(s, d, small_sem.at[i])
        for i, (s, d) in enumerate(
            ((nsc_h, nsc), (nsh_h, nsh), (be_h, be), (dk_h, dk), (db_h, db), (bp_h, bp),
             (ag_h, ag), (as_h, ash), (bq_h, bq), (bo_h, bo))
        )
    ]
    for s in smalls:
        s.start()
    wide = E // WCHUNKS
    wcopies = [
        pltpu.make_async_copy(
            we_h.at[:, pl.ds(i * wide, wide)], we.at[:, pl.ds(i * wide, wide)], we_sem.at[i]
        )
        for i in range(WCHUNKS)
    ]
    for w in wcopies:
        w.start()

    def signal(i, _):
        pl.semaphore_signal(
            bar, inc=1, device_id=place(lax.rem(me + i, PEERS)), device_id_type=MESH
        )
        return 0

    lax.fori_loop(1, PEERS, signal, 0, unroll=9)
    for dr in (-1, 0, 1):
        for dc in (-1, 1):
            pl.semaphore_signal(
                bar, inc=1,
                device_id=(lax.rem(r + dr + ROWS, ROWS), lax.rem(c + dc + COLS, COLS)),
                device_id_type=MESH,
            )

    fcopy.wait()
    for s in smalls:
        s.wait()

    def normalise(v):
        return (v.astype(F32) * nsc[...][None, :] + nsh[...][None, :]).astype(BF16)

    def norm_row(h, _):
        xn[pl.ds(pl.multiple_of(h * TC, TC), TC), :] = normalise(feat[h])
        return 0

    lax.fori_loop(0, TR, norm_row, 0)

    def expand_chunk(ci, _):
        cols = pl.ds(pl.multiple_of(ci * 256, 256), 256)
        for mb in range(2):
            acc = jnp.dot(
                xn[mb * 256 : (mb + 1) * 256, :], we[:, cols], preferred_element_type=F32
            )
            g = gelu(acc + be[:, cols]).astype(BF16)
            hid[1 + 4 * mb : 5 + 4 * mb, :, cols] = g.reshape(4, TC, 256)
        return 0

    early = 1
    for i in range(early):
        wcopies[i].wait()
        lax.fori_loop(2 * i, 2 * i + 2, expand_chunk, 0, unroll=2)

    bigs = [
        pltpu.make_async_copy(s, d, w_sem.at[i])
        for i, (s, d) in enumerate(((wp_h, wp), (wq_h, wq), (wo_h, wo)))
    ]
    for w in bigs:
        w.start()

    pl.semaphore_wait(bar, PEERS - 1 + 6)

    def halo(src, dst, k, dr, dc):
        return pltpu.make_async_remote_copy(
            src_ref=src, dst_ref=dst, send_sem=halo_ssem.at[k], recv_sem=halo_rsem.at[k],
            device_id=(lax.rem(r + dr + ROWS, ROWS), lax.rem(c + dc + COLS, COLS)),
            device_id_type=MESH,
        )

    halos = [
        halo(feat.at[TR - 1], top, 0, 1, 0),
        halo(feat.at[0], bot, 1, -1, 0),
        halo(feat.at[:, pl.ds(TC - 4, 4)], left.at[:, pl.ds(4, 4)], 2, 0, 1),
        halo(feat.at[:, pl.ds(0, 4)], right.at[:, pl.ds(0, 4)], 3, 0, -1),
        halo(feat.at[TR - 1, pl.ds(TC - 4, 4)], corner.at[0, pl.ds(4, 4)], 4, 1, 1),
        halo(feat.at[0, pl.ds(TC - 4, 4)], corner.at[1, pl.ds(4, 4)], 5, -1, 1),
        halo(feat.at[TR - 1, pl.ds(0, 4)], corner.at[2, pl.ds(0, 4)], 6, 1, -1),
        halo(feat.at[0, pl.ds(0, 4)], corner.at[3, pl.ds(0, 4)], 7, -1, -1),
    ]
    for h in halos:
        h.start()

    for i in range(early, WCHUNKS):
        wcopies[i].wait()
        lax.fori_loop(2 * i, 2 * i + 2, expand_chunk, 0, unroll=2)

    for h in halos:
        h.wait()

    top_ok = jnp.where(r > 0, 1.0, 0.0).astype(F32)
    bot_ok = jnp.where(r < ROWS - 1, 1.0, 0.0).astype(F32)
    left_ok = jnp.where(c > 0, 1.0, 0.0).astype(F32)
    right_ok = jnp.where(c < COLS - 1, 1.0, 0.0).astype(F32)

    xn[0:TC, :] = normalise(top[...])
    xn[TC : 2 * TC, :] = normalise(bot[...])
    for i in range(TR):
        xblk[i * 8 : i * 8 + 8, :] = normalise(left[i])
        xblk[64 + i * 8 : 64 + i * 8 + 8, :] = normalise(right[i])
    for i in range(4):
        xblk[128 + i * 8 : 136 + i * 8, :] = normalise(corner[i])
    xblk[160:256, :] = jnp.zeros((96, C), BF16)
    t = lax.broadcasted_iota(jnp.int32, (32, 256), 0)
    n = lax.broadcasted_iota(jnp.int32, (32, 256), 1)
    tr = lax.rem(t, 16)
    want_l = jnp.where(tr == 0, 135, jnp.where(tr == 9, 143, (tr - 1) * 8 + 7))
    want_r = jnp.where(tr == 0, 144, jnp.where(tr == 9, 152, 64 + (tr - 1) * 8))
    want = jnp.where(t < 16, want_l, want_r)
    want = jnp.where(tr <= 9, want, -1)
    pick = jnp.where(n == want, 1.0, 0.0).astype(BF16)
    xn[2 * TC : 2 * TC + 32, :] = jnp.dot(
        pick, xblk[...], preferred_element_type=F32
    ).astype(BF16)

    def halo_chunk(ci, _):
        cols = pl.ds(pl.multiple_of(ci * 256, 256), 256)
        acc = jnp.dot(xn[0 : 2 * TC + 32, :], we[:, cols], preferred_element_type=F32)
        g = gelu(acc + be[:, cols])
        hid[0, :, cols] = (g[0:TC] * top_ok).astype(BF16)
        hid[TR + 1, :, cols] = (g[TC : 2 * TC] * bot_ok).astype(BF16)
        gs = g[2 * TC : 2 * TC + 32].astype(BF16).astype(F32)
        ti = lax.broadcasted_iota(jnp.int32, (16, 256), 0)
        edge = jnp.where(ti == 0, top_ok, jnp.where(ti == 9, bot_ok, 1.0))
        gl = gs[0:16] * (edge * left_ok)
        gr = gs[16:32] * (edge * right_ok)
        kl = [dk[a, 0:1, cols] for a in range(3)]
        kr = [dk[a, 2:3, cols] for a in range(3)]
        ledge = gl[0:8] * kl[0] + gl[1:9] * kl[1] + gl[2:10] * kl[2]
        redge = gr[0:8] * kr[0] + gr[1:9] * kr[1] + gr[2:10] * kr[2]
        for i in range(TR):
            hl[i, :, cols] = jnp.broadcast_to(ledge[i : i + 1], (8, 256))
            hr[i, :, cols] = jnp.broadcast_to(redge[i : i + 1], (8, 256))
        return 0

    lax.fori_loop(0, E // 256, halo_chunk, 0, unroll=6)

    bigs[0].wait()
    sub_id = lax.broadcasted_iota(jnp.int32, (8, 128), 0)

    def send_chunk(p):
        return pltpu.make_async_remote_copy(
            src_ref=send.at[p], dst_ref=recv.at[me], send_sem=a_ssem, recv_sem=a_rsem,
            device_id=place(p), device_id_type=MESH,
        )

    def block(k, _):
        b = (k + (me >> 4)) & 3

        def depthwise(ci):
            for half in range(2):
                cols = pl.ds(pl.multiple_of(ci * 256 + half * 128, 128), 128)
                rows = [hid[2 * b + i, :, cols].astype(F32) for i in range(4)]
                bias = db[:, cols]
                taps = [[dk[a, q : q + 1, cols] for q in range(3)] for a in range(3)]
                for o in range(2):
                    s = [
                        rows[o] * taps[0][q] + rows[o + 1] * taps[1][q] + rows[o + 2] * taps[2][q]
                        for q in range(3)
                    ]
                    down = pltpu.roll(s[0], 1, 0)
                    up = pltpu.roll(s[2], TC - 1, 0)
                    first = jnp.where(sub_id == 0, hl[2 * b + o, :, cols], down[0:8])
                    last = jnp.where(sub_id == 7, hr[2 * b + o, :, cols], up[TC - 8 : TC])
                    total = (
                        s[1] + bias
                        + jnp.concatenate([first, down[8:TC]], axis=0)
                        + jnp.concatenate([up[0 : TC - 8], last], axis=0)
                    )
                    dwb[o * TC : (o + 1) * TC, cols] = gelu(total.astype(BF16))

        def project(ci):
            part = pl.ds(pl.multiple_of(ci * 256, 256), 256)
            acc[...] += jnp.dot(dwb[:, part], wp[part, :], preferred_element_type=F32)

        def lane(ci, _):
            project(ci - 1)
            depthwise(ci)
            return 0

        acc[...] = jnp.broadcast_to(bp[...][None, :], (2 * TC, C))
        depthwise(0)
        lax.fori_loop(1, E // 256, lane, 0)
        project(E // 256 - 1)
        proj = acc[...]
        f0 = feat[2 * b].astype(F32)
        f1 = feat[2 * b + 1].astype(F32)
        for o, f in ((0, f0), (1, f1)):
            acb = (f + proj[o * TC : (o + 1) * TC]).astype(BF16)
            feat[2 * b + o] = acb
            wide_ac = acb.astype(F32)
            center = wide_ac - jnp.mean(wide_ac, axis=-1, keepdims=True)
            spread = jnp.mean(center * center, axis=-1, keepdims=True)
            y = (center * lax.rsqrt(spread + 1e-06) * ag[...][None, :] + ash[...][None, :]).astype(BF16)
            send[pl.ds((2 * b + o) * 8, 8)] = y.reshape(8, 8, C)

        def go(j, _):
            p = 16 * b + lax.rem(j + me, 16)

            @pl.when(p != me)
            def _():
                send_chunk(p).start()

            return 0

        lax.fori_loop(0, 16, go, 0, unroll=16)
        return 0

    lax.fori_loop(0, 4, block, 0)
    accopy = pltpu.make_async_copy(feat, ac_out, out_sem)
    accopy.start()
    recv[pl.ds(me, 1)] = send[pl.ds(me, 1)]
    ri = lax.broadcasted_iota(jnp.int32, (256, 256), 0) >> 6
    rj = lax.broadcasted_iota(jnp.int32, (256, 256), 1) >> 6
    ones[...] = jnp.where(ri == rj, 1.0, 0.0).astype(BF16)
    bigs[1].wait()
    bigs[2].wait()
    pltpu.make_async_copy(send.at[pl.ds(0, PEERS - 1)], send.at[pl.ds(0, PEERS - 1)], a_ssem).wait()
    pltpu.make_async_copy(recv.at[pl.ds(0, PEERS - 1)], recv.at[pl.ds(0, PEERS - 1)], a_rsem).wait()

    lane_head = lax.broadcasted_iota(jnp.int32, (64, 128), 1) >> 5
    masks = [jnp.where(lane_head == i, 1.0, 0.0).astype(BF16) for i in range(4)]

    def return_chunk(p, sub):
        return pltpu.make_async_remote_copy(
            src_ref=retbuf.at[sub, p], dst_ref=ret_out.at[me, pl.ds(PER * sub, PER)],
            send_sem=b_ssem, recv_sem=b_rsem, device_id=place(p), device_id_type=MESH,
        )

    subrows = PER * PEERS

    for sub in range(NSUB):
        m = lax.broadcasted_iota(jnp.int32, (subrows, TOKENS), 0)
        nn = lax.broadcasted_iota(jnp.int32, (subrows, TOKENS), 1)
        perm = jnp.where(nn == (m & 63) * 8 + (m >> 6) + PER * sub, 1.0, 0.0).astype(BF16)
        xp[...] = jnp.dot(
            perm, recv[...].reshape(TOKENS, C), preferred_element_type=F32
        ).astype(BF16)

        def qkv_chunk(ci, _):
            cols = pl.ds(pl.multiple_of(ci * 256, 256), 256)
            part = jnp.dot(xp[...], wq[:, cols], preferred_element_type=F32)
            qkv[:, cols] = (part + bq[cols][None, :]).astype(BF16)
            if sub > 0:
                for j in range(7):
                    return_chunk((ci * 7 + j + 1 + me) & (PEERS - 1), sub - 1).start()
            return 0

        lax.fori_loop(0, 9, qkv_chunk, 0, unroll=9)

        def group(g, _):
            rows = pl.ds(pl.multiple_of(g * 64, 64), 64)
            es = []
            for quad in range(QUADS):
                lo = quad * 128
                q = qkv[rows, lo : lo + 128]
                kk = qkv[rows, C + lo : C + lo + 128]
                kbd = jnp.concatenate([kk * m for m in masks], axis=0)
                s = lax.dot_general(
                    q, kbd, (((1,), (1,)), ((), ())), preferred_element_type=F32
                )
                es.append(jnp.exp2(s * EXP_SCALE))
            e = jnp.concatenate(es, axis=0)
            tot = jnp.dot(e.astype(BF16), ones[...], preferred_element_type=F32)
            probs = (e / tot).astype(BF16)
            for quad in range(QUADS):
                lo = quad * 128
                vv = qkv[rows, 2 * C + lo : 2 * C + lo + 128]
                vbd = jnp.concatenate([vv * m for m in masks], axis=0)
                o = jnp.dot(
                    probs[quad * 64 : (quad + 1) * 64], vbd, preferred_element_type=F32
                )
                mixed[rows, lo : lo + 128] = o.astype(BF16)
            return 0

        lax.fori_loop(0, PER, group, 0, unroll=4)
        parts = 2 if sub == NSUB - 1 else 1
        span, peers = subrows // parts, PEERS // parts
        m = lax.broadcasted_iota(jnp.int32, (span, subrows), 0)
        nn = lax.broadcasted_iota(jnp.int32, (span, subrows), 1)
        for part in range(parts):
            which = (part + me) & (parts - 1)
            token = m + which * span
            back = jnp.where(
                nn == (token & (PER - 1)) * 64 + (token >> PER_BITS), 1.0, 0.0
            ).astype(BF16)
            mm = jnp.dot(back, mixed[...], preferred_element_type=F32).astype(BF16)
            y = (jnp.dot(mm, wo[...], preferred_element_type=F32) + bo[...][None, :]).astype(BF16)
            retbuf[sub, pl.ds(which * peers, peers)] = y.reshape(peers, PER, C)

            def go(j, _):
                p = which * peers + ((j + me) & (peers - 1))

                @pl.when(p != me)
                def _():
                    return_chunk(p, sub).start()

                return 0

            if sub == NSUB - 1:
                lax.fori_loop(0, peers, go, 0, unroll=32)
        pltpu.make_async_copy(
            retbuf.at[sub, me], ret_out.at[me, pl.ds(PER * sub, PER)], self_sem.at[sub]
        ).start()

    for sub in range(NSUB):
        pltpu.make_async_copy(
            retbuf.at[sub, me], ret_out.at[me, pl.ds(PER * sub, PER)], self_sem.at[sub]
        ).wait()
    accopy.wait()
    pltpu.make_async_copy(ret_out.at[pl.ds(0, PEERS - 1)], ret_out.at[pl.ds(0, PEERS - 1)], b_ssem).wait()
    pltpu.make_async_copy(ret_out.at[pl.ds(0, PEERS - 1)], ret_out.at[pl.ds(0, PEERS - 1)], b_rsem).wait()


def per_device(
    features, norm_scale, norm_shift, expand_weight, expand_bias, depth_kernel, depth_bias,
    project_weight, project_bias, attn_gain, attn_shift, qkv_weight, qkv_bias, out_weight, out_bias,
):
    row = lambda v: v if v.shape[0] % 1024 else v.reshape(1, -1)
    args = (
        features, row(norm_scale), row(norm_shift), expand_weight, row(expand_bias), depth_kernel,
        row(depth_bias), project_weight, row(project_bias), row(attn_gain), row(attn_shift),
        qkv_weight, row(qkv_bias), out_weight, row(out_bias),
    )
    vm = pltpu.VMEM
    dma = pltpu.SemaphoreType.DMA
    scratch = [vm(a.shape, a.dtype) for a in args]
    scratch += [
        vm((TOKENS, C), BF16),
        vm((TC, C), BF16),
        vm((TC, C), BF16),
        vm((TR, 8, C), BF16),
        vm((TR, 8, C), BF16),
        vm((4, 8, C), BF16),
        vm((256, C), BF16),
        vm((TR + 2, TC, E), BF16),
        vm((TR, 8, E), F32),
        vm((TR, 8, E), F32),
        vm((2 * TC, E), BF16),
        vm((PEERS, 8, C), BF16),
        vm((PEERS, 8, C), BF16),
        vm((TOKENS // NSUB, C), BF16),
        vm((TOKENS // NSUB, 3 * C), BF16),
        vm((TOKENS // NSUB, C), BF16),
        vm((NSUB, PEERS, PER, C), BF16),
        vm((2 * TC, C), F32),
        vm((256, 256), BF16),
        dma((10,)), dma, dma((WCHUNKS,)), dma((3,)), dma((8,)), dma((8,)),
        dma, dma, dma, dma, dma, dma((NSUB,)),
    ]
    hbm = pl.BlockSpec(memory_space=pl.ANY)
    after_conv, attended = pl.pallas_call(
        kernel,
        out_shape=(
            jax.ShapeDtypeStruct((TR, TC, C), BF16),
            jax.ShapeDtypeStruct((PEERS, 8, C), BF16),
        ),
        in_specs=[hbm] * len(args),
        out_specs=(hbm, hbm),
        scratch_shapes=scratch,
        name="block",
        compiler_params=pltpu.CompilerParams(
            collective_id=0, has_side_effects=True, vmem_limit_bytes=60 << 20
        ),
    )(*args)
    return (after_conv.astype(F32) + attended.reshape(after_conv.shape).astype(F32)).astype(BF16)


def solution(mesh):
    return jax.shard_map(
        per_device,
        mesh=mesh,
        in_specs=(P("row", "col", None),) + (P(),) * 14,
        out_specs=P("row", "col", None),
        check_vma=False,
    )
```
